32 devices in a mesh: depth: 4 (over x, core), tile: 8 (over z, y).
Axes of the slice: x: 2, y: 2, z: 4, core: 2. Of those that a mesh axis runs over, the one named last changes fastest.
Arguments:
- volume: bfloat16 [512, 64, 64, 64], P(('depth', 'tile')), may hold values from 0.0099487305 to 0.5
- resampler: bfloat16 [2, 64, 128], replicated, may hold values from 0 to 1.4, as said below
- ramp_slope: float32 [3], replicated, may hold values from -12 to 12
- ramp_pivot: float32 [3], replicated, may hold values from 0.03 to 0.3
- tile_owner: int32 [512, 2], P(('depth', 'tile')), may hold values from 0 to 7, all different within a row; in each aligned block of 16 rows (0 to 15, 16 to 31, ...) at most 8 rows name the same one
- tile_cell: int32 [512, 2], P(('depth', 'tile')), may hold values from 0 to 7
- depth_order: int32 [2, 512], P(None, ('depth', 'tile')), may hold values from 0 to 511, each once within a row
- slab_rank: int32 [2, 4], replicated, may hold values from 0 to 3, each once within a row
Outputs:
- colour: float32 [2, 3, 8, 512, 128], P(None, None, 'tile', 'depth')
- transmittance: float32 [2, 8, 512, 128], P(None, 'tile', 'depth')
The draws below stay inside these ranges and needn't reach their ends.
Inputs may be any that keep to these rules, and one draw needn't show every extreme that they name: `tile_owner`: each row names 2 different tile owners. Among the 16 rows of one device no owner is named by more than 8 rows, a bound that some block reaches. `depth_order`: each row is a permutation. `slab_rank`: each row is a permutation. `resampler`: nonnegative interpolation weights.
All inputs are finite; a program needn't handle non-finite values.
Results may differ from the reference program's by a relative error of at most 0.0025.
Values may be sent and summed in bfloat16 or wider, within the bound.
No kernel may reach another device: no remote copies, remote signals or barrier semaphores. Data moves between devices by JAX's collectives and lax.ppermute only.
A program may use at most 128 MiB of HBM per device.

```python
import math
import jax
import jax.numpy as jnp
import numpy as np
from jax import lax

BRICK = 64
SAMPLES = 128
CELLS = 8
VIEWS = 2
BRICKS_DEV = 16
TILES = 8
SLABS = 4
BRICKS = 512
CAP = 8


def draw_resampler(key, part):
    subkeys = jax.random.split(key, 2)
    shear_offset = jax.random.uniform(subkeys[0], (VIEWS, 1, 1), minval=-0.5, maxval=0.5)
    jitter = 0.25
    roughness = jax.random.uniform(subkeys[1], (VIEWS, BRICK, SAMPLES), minval=-1.0, maxval=1.0)
    voxel_pos = jnp.arange(BRICK, dtype=jnp.float32)[None, :, None]
    sample_pos = (jnp.arange(SAMPLES, dtype=jnp.float32)[None, None, :] + 0.5) * (BRICK / SAMPLES) - 0.5 + shear_offset
    tent_weight = jnp.maximum(0.0, 1.0 - jnp.abs(voxel_pos - sample_pos))
    return (tent_weight * (1.0 + jitter * roughness)).astype(jnp.bfloat16)


def touch_ends(drawn, stream_key, least, largest):
    shape = drawn.shape
    index_at = [jax.random.randint(jax.random.fold_in(stream_key, axis), (), 0, shape[axis]) for axis in range(len(shape))]
    drawn = drawn.at[tuple(index_at)].set(least)
    longest = shape.index(max(shape))
    index_at[longest] = (index_at[longest] + 1) % shape[longest]
    return drawn.at[tuple(index_at)].set(largest)


def shard_levels(stream_key, dims, cuts, smallest, high):
    def one(position, parts):
        heights = jax.random.uniform(jax.random.fold_in(jax.random.fold_in(stream_key, 6), position), (parts,), jnp.float32, smallest / len(cuts), high / len(cuts))
        return jnp.repeat(jnp.exp(heights), dims[position] // parts).reshape((-1,) + (1,) * (len(dims) - position - 1))

    gain = one(*cuts[0])
    for cut in cuts[1:]:
        gain = gain * one(*cut)
    return gain


def shared_out(own_key, own, number, rows, count, top, bound, skew):
    sequence = jax.random.permutation(own_key, count)
    heavy_load, common = shares(count, rows * top, bound, skew, True), shares(count, rows * top, bound, skew, False)
    places = jnp.arange(count)

    def named(tallies, rotation):
        used = int((tallies > 0).sum())
        fixed = max(1, used // 4)
        shifted = fixed + (places - fixed + rotation * (used - fixed)) % max(1, count - fixed)
        return jnp.zeros((count,), jnp.int32).at[sequence[jnp.where(places < fixed, places, shifted)]].set(jnp.asarray(tallies, jnp.int32))

    tallies = jnp.where(number % 4 == 0, named(heavy_load, number // 4), named(common, number - number // 4 - 1))
    mixed = jax.random.permutation(jax.random.fold_in(own, 3), count)
    source_of, taker = mixed[0:count // 2 * 2:2], mixed[1:count // 2 * 2:2]
    slack = jnp.minimum(tallies[source_of] - 1, bound - tallies[taker]) // 2
    slack = jnp.where((source_of == sequence[0]) | (taker == sequence[0]) | (tallies[taker] == 0), 0, jnp.maximum(slack, 0))
    shifted = jax.random.randint(jax.random.fold_in(own, 4), (count // 2,), 0, 1 << 20) % (slack + 1)
    tallies = tallies.at[source_of].add(-shifted).at[taker].add(shifted)
    items = jnp.searchsorted(jnp.cumsum(tallies), jnp.arange(rows * top), side="right").astype(jnp.int32)
    table = items.reshape(top, rows).T
    table = table[jax.random.permutation(jax.random.fold_in(own, 1), rows)]
    rotation = jax.random.randint(jax.random.fold_in(own, 2), (rows, 1), 0, top)
    return jnp.take_along_axis(table, (jnp.arange(top)[None, :] + rotation) % top, axis=1)


def shares(amount, total, reach, slope, full):
    portions = [(1 << 20) // math.isqrt(standing ** slope) + 1 for standing in range(1, amount + 1)]
    largest = reach if full else min(reach, max(-(-total // amount), total * portions[0] // sum(portions)))
    least = 1 if total - largest >= amount - 1 else 0
    given, rest = [largest] + [least] * (amount - 1), total - largest - least * (amount - 1)
    while rest > 0:
        candidates = [i for i in range(1, amount) if given[i] < largest] or [i for i in range(1, amount) if given[i] < reach]
        mass, remaining = sum([portions[i] for i in candidates]), rest
        for i in candidates:
            more = min(reach - given[i], max(1, remaining * portions[i] // mass), rest)
            given[i] = given[i] + more
            rest = rest - more
    return np.array(given)


def setup_inputs(seed: int = 0) -> dict:
    splits = jax.random.split(jax.random.key(seed), 9)
    volume = jnp.clip(jnp.exp(math.log(0.5) - 3.9171631 * jax.random.uniform(splits[0], (BRICKS, BRICK, BRICK, BRICK), jnp.float32) ** shard_levels(splits[0], (BRICKS, BRICK, BRICK, BRICK), ((0, 32),), -0.2, 0.2)), 0.0099487305, 0.5).astype(jnp.bfloat16)
    resampler = draw_resampler(jax.random.fold_in(splits[8], 71), 0)
    ramp_slope = jnp.clip(jax.random.uniform(splits[2], (3,), jnp.float32, -12.0, 12.0), -12.0, 12.0)
    ramp_pivot = jnp.clip(jax.random.uniform(splits[3], (3,), jnp.float32, 0.03, 0.3), 0.03, 0.3)
    tile_owner_keys = jax.random.split(jax.random.fold_in(splits[4], 1), BRICKS // BRICKS_DEV)
    tile_owner_turns = jax.random.permutation(jax.random.fold_in(splits[4], 3), BRICKS // BRICKS_DEV)
    tile_owner = jax.vmap(lambda own, number: shared_out(jax.random.fold_in(splits[4], 2), own, number, BRICKS_DEV, TILES, VIEWS, CAP, 2))(tile_owner_keys, tile_owner_turns).reshape((BRICKS, VIEWS))
    tile_cell = touch_ends(jax.random.randint(splits[5], (BRICKS, VIEWS), 0, CELLS), jax.random.fold_in(splits[5], 1), 0, CELLS - 1).astype(jnp.int32)
    depth_order = jax.vmap(lambda own: jax.random.permutation(own, BRICKS))(jax.random.split(splits[6], VIEWS)).reshape((VIEWS, BRICKS)).astype(jnp.int32)
    slab_rank = jax.vmap(lambda own: jax.random.permutation(own, SLABS))(jax.random.split(splits[7], VIEWS)).reshape((VIEWS, SLABS)).astype(jnp.int32)
    return dict(volume=volume, resampler=resampler, ramp_slope=ramp_slope, ramp_pivot=ramp_pivot, tile_owner=tile_owner, tile_cell=tile_cell, depth_order=depth_order, slab_rank=slab_rank)


EXTINCTION = 1.0
TOP_PRECISION = lax.Precision.HIGHEST


def render_brick(brick, resampler, ramp_slope, ramp_pivot):
    cube = brick.astype(jnp.float32)
    weights = resampler.astype(jnp.float32)
    rowwise_axis = jnp.einsum("kri,is->krs", cube, weights[0], precision=TOP_PRECISION)
    along_depth = jnp.einsum("rik,is->krs", cube, weights[1], precision=TOP_PRECISION)
    samples = jnp.stack([rowwise_axis, along_depth])
    optical = samples * (EXTINCTION / samples.shape[1])
    nearest_depth = jnp.cumsum(optical, axis=1) - optical
    weight = jnp.exp(-nearest_depth) * (1.0 - jnp.exp(-optical))
    layers = []
    for channel in range(3):
        tinted = jax.nn.sigmoid(ramp_slope[channel] * (samples - ramp_pivot[channel]))
        layers.append(jnp.sum(weight * tinted, axis=1))
    layers.append(jnp.sum(optical, axis=1))
    return jnp.stack(layers, axis=1)


def compose_slab(prints, owners, cells, ranks):
    tiles_out = []
    for view_index in range(2):
        flat_prints = prints[:, view_index]
        brick_count = flat_prints.shape[0]
        target = owners[:, view_index] * CELLS + cells[:, view_index]
        rank_tag = ranks[view_index]
        before = (target[None, :] == target[:, None]) & (rank_tag[None, :] < rank_tag[:, None])
        depth_values = flat_prints[:, 3].reshape(brick_count, -1)
        nearest_depth = jnp.dot(before.astype(jnp.float32), depth_values, precision=TOP_PRECISION)
        nearest_depth = nearest_depth.reshape(flat_prints[:, 3].shape)
        lit_colour = flat_prints[:, :3] * jnp.exp(-nearest_depth)[:, None]
        combined_result = jnp.concatenate([lit_colour, flat_prints[:, 3:]], axis=1)
        summed = jax.ops.segment_sum(combined_result, target, num_segments=TILES * CELLS)
        summed = summed.reshape(TILES, CELLS, 4, BRICK, SAMPLES).transpose(0, 2, 1, 3, 4)
        tiles_out.append(summed.reshape(TILES, 4, CELLS * BRICK, SAMPLES))
    return jnp.stack(tiles_out).astype(jnp.bfloat16)


def reference(volume, resampler, ramp_slope, ramp_pivot, tile_owner, tile_cell, depth_order, slab_rank):
    slab_bricks = BRICKS_DEV * TILES

    def one_slab(slab):
        start = (slab * slab_bricks).astype(jnp.int32)
        cubes = lax.dynamic_slice_in_dim(volume, start, slab_bricks, 0)
        owners = lax.dynamic_slice_in_dim(tile_owner, start, slab_bricks, 0)
        cells = lax.dynamic_slice_in_dim(tile_cell, start, slab_bricks, 0)
        ranks = lax.dynamic_slice_in_dim(depth_order, start, slab_bricks, 1)
        prints = lax.map(lambda brick: render_brick(brick, resampler, ramp_slope, ramp_pivot), cubes)
        return compose_slab(prints, owners, cells, ranks)

    slab_tiles = lax.map(one_slab, jnp.arange(SLABS, dtype=jnp.int32)).astype(jnp.float32)
    is_nearer = (slab_rank[:, None, :] < slab_rank[:, :, None]).astype(jnp.float32)
    depth_values = slab_tiles[:, :, :, 3]
    nearest_depth = jnp.einsum("jeh,hjxqg->ejxqg", is_nearer, depth_values, precision=TOP_PRECISION)
    colour = jnp.sum(jnp.exp(-nearest_depth)[:, :, :, None] * slab_tiles[:, :, :, :3], axis=0)
    colour = colour.transpose(0, 2, 1, 3, 4)
    transmittance = jnp.exp(-jnp.sum(depth_values, axis=0))
    return (colour, transmittance)
```

```python
import functools

import jax
import jax.numpy as jnp
from jax import lax
from jax.experimental import pallas as pl
from jax.experimental.pallas import tpu as pltpu
from jax.sharding import PartitionSpec as P

LOG2E = 1.4426950408889634
GROUP = 8
CELLS = 8
AXES = ("depth", "tile")


def render_kernel(slope_ref, pivot_ref, vol_ref, res_ref, out_ref, even_ref, odd_ref, ramp_ref, acc_ref, seen_ref, tint_ref, print_ref, *, view):
    step = pl.program_id(0)
    bricks = pl.num_programs(0) - 1
    edge = vol_ref.shape[1]
    cols = res_ref.shape[1]
    blocks = edge // GROUP
    half = edge // 2
    rate = -LOG2E / edge

    def multiply(block, samp_ref):
        if view == 0:
            rows = vol_ref[0, pl.ds(block * GROUP, GROUP)].reshape(GROUP * edge, edge)
            made = jnp.dot(rows, res_ref[...], preferred_element_type=jnp.float32)
            samp_ref[pl.ds(block * GROUP * edge, GROUP * edge), :] = made
        else:
            for j in range(GROUP):
                made = lax.dot_general(
                    vol_ref[0, block * GROUP + j], res_ref[...], (((0,), (0,)), ((), ())),
                    preferred_element_type=jnp.float32)
                samp_ref[pl.ds(block * GROUP * (edge + 1) + j * (edge + 1), edge), :] = made

    def start():
        acc_ref[...] = jnp.zeros_like(acc_ref)
        seen_ref[...] = jnp.ones_like(seen_ref)
        tint_ref[...] = jnp.zeros_like(tint_ref)

    def ramps():
        for ch in range(3):
            gain = jnp.full((16, cols), 0.5 * slope_ref[ch], jnp.float32)
            offset = -gain * pivot_ref[ch]
            for place, value in ((0, gain), (1, offset)):
                debt = jnp.zeros_like(value)
                for j in range(GROUP):
                    want = value + debt
                    given = want.astype(jnp.bfloat16)
                    debt = want - given.astype(jnp.float32)
                    ramp_ref[j, ch, place] = given

    def march(block, samp_ref):
        for top in range(0, edge, half):
            acc = acc_ref[pl.ds(top, half), :]
            seen = seen_ref[pl.ds(top, half), :]
            part = [[] for _ in range(3)]
            for j in range(GROUP):
                if view == 0:
                    s = samp_ref[pl.ds((block * GROUP + j) * edge + top, half), :]
                else:
                    s = samp_ref[pl.ds(top * (edge + 1) + block * GROUP + j, half, stride=edge + 1), :]
                acc = acc + s
                left = jnp.exp2(acc * rate)
                w = (seen - left).astype(jnp.bfloat16)
                seen = left
                s16 = s.astype(jnp.bfloat16)
                for ch in range(3):
                    gain = jnp.concatenate([ramp_ref[j, ch, 0]] * (half // 16), axis=0)
                    offset = jnp.concatenate([ramp_ref[j, ch, 1]] * (half // 16), axis=0)
                    p = w * jnp.tanh(s16 * gain + offset)
                    n = j
                    while n % 2 == 1:
                        p = part[ch].pop() + p
                        n //= 2
                    part[ch].append(p)
            for ch in range(3):
                tint_ref[ch, pl.ds(top, half), :] += part[ch][0].astype(jnp.float32)
            acc_ref[pl.ds(top, half), :] = acc
            seen_ref[pl.ds(top, half), :] = seen

    def finish(brick):
        alpha = 1.0 - seen_ref[...]
        for ch in range(3):
            print_ref[pl.ds((ch * bricks + brick) * (edge + 1), edge), :] = 0.5 * (alpha + tint_ref[ch])
        print_ref[pl.ds((3 * bricks + brick) * (edge + 1), edge), :] = acc_ref[...] * (1.0 / edge)

    def loop(f):
        def it(block, carry):
            f(block)
            return carry
        lax.fori_loop(0, blocks, it, 0)

    @pl.when(step == 0)
    def _():
        ramps()
        loop(lambda block: multiply(block, even_ref))

    for parity, (own, other) in enumerate(((even_ref, odd_ref), (odd_ref, even_ref))):
        @pl.when((step > 0) & (step < bricks) & (lax.rem(step, 2) == parity))
        def _():
            start()

            def both(block):
                multiply(block, own)
                march(block, other)
            loop(both)
            finish(step - 1)

    last = odd_ref if last_slot_is_odd(out_ref) else even_ref

    @pl.when(step == bricks)
    def _():
        start()
        loop(lambda block: march(block, last))
        finish(step - 1)

        def swap(row, carry):
            out_ref[row] = print_ref[pl.ds(row, out_ref.shape[1], stride=edge + 1), :].astype(jnp.bfloat16)
            return carry
        lax.fori_loop(0, edge, swap, 0, unroll=4)


def last_slot_is_odd(out_ref):
    return (out_ref.shape[1] // 4 - 1) % 2 == 1


def render(volume, resampler, slope, pivot, view, first, count):
    edge, cols = volume.shape[1], resampler.shape[1]
    smem = pl.BlockSpec(memory_space=pltpu.SMEM)
    return pl.pallas_call(
        functools.partial(render_kernel, view=view),
        grid=(count + 1,),
        in_specs=[
            smem, smem,
            pl.BlockSpec((1, edge, edge, edge), lambda g: (first + jnp.minimum(g, count - 1), 0, 0, 0)),
            pl.BlockSpec((edge, cols), lambda g: (0, 0)),
        ],
        out_specs=pl.BlockSpec((edge, 4 * count, cols), lambda g: (0, 0, 0)),
        out_shape=jax.ShapeDtypeStruct((edge, 4 * count, cols), jnp.bfloat16),
        scratch_shapes=[
            pltpu.VMEM((edge * (edge + 1), cols), jnp.float32),
            pltpu.VMEM((edge * (edge + 1), cols), jnp.float32),
            pltpu.VMEM((GROUP, 3, 2, 16, cols), jnp.bfloat16),
            pltpu.VMEM((edge, cols), jnp.float32),
            pltpu.VMEM((edge, cols), jnp.float32),
            pltpu.VMEM((3, edge, cols), jnp.float32),
            pltpu.VMEM((4 * count * (edge + 1), cols), jnp.float32),
        ],
        name=f"render{view}",
    )(slope, pivot, volume, resampler)


def compose_kernel(row_ref, col_ref, *refs, base, halves):
    got, out_ref, feat_ref, sum_ref = refs[:halves], refs[halves], refs[halves + 1], refs[halves + 2]
    total, cols = feat_ref.shape[1:]
    places = sum_ref.shape[1]
    sources, _, slots, _ = got[0].shape
    bricks = slots // 4
    piece = sources * bricks
    for h in range(halves):
        for ch in range(4):
            part = got[h][:, 0, ch * bricks:(ch + 1) * bricks, :].astype(jnp.float32)
            feat_ref[ch, h * piece:(h + 1) * piece, :] = part.reshape(piece, cols).astype(jnp.bfloat16)
    sum_ref[...] = jnp.zeros_like(sum_ref)
    block = min(256, total)
    row = row_ref[...]
    start = lax.broadcasted_iota(jnp.int32, (places, block), 0) * base

    def it(i, carry):
        rows = pl.ds(i * block, block)
        code = col_ref[rows, 0:1]
        floor = col_ref[rows, 1:2]
        before = ((row >= floor) & (row < code)).astype(jnp.float32).astype(jnp.bfloat16)
        inner = jnp.dot(before, feat_ref[3], preferred_element_type=jnp.float32)
        light = jnp.exp(-inner)
        own = row_ref[:, rows]
        pick = ((own >= start) & (own < start + base)).astype(jnp.float32).astype(jnp.bfloat16)
        for ch in range(4):
            value = feat_ref[ch, rows, :]
            if ch < 3:
                value = (value.astype(jnp.float32) * light).astype(jnp.bfloat16)
            sum_ref[ch] += jnp.dot(pick, value, preferred_element_type=jnp.float32)
        return carry

    lax.fori_loop(0, total // block, it, 0)
    for ch in range(3):
        out_ref[:, 0, ch, :] = sum_ref[ch]
    out_ref[:, 0, 3, :] = jnp.exp(-sum_ref[3])


def compose(row, col, got, places, base):
    sources, bands, slots, cols = got[0].shape
    total = row.shape[1]
    halves = len(got)
    return pl.pallas_call(
        functools.partial(compose_kernel, base=base, halves=halves),
        grid=(bands,),
        in_specs=[
            pl.BlockSpec((1, total), lambda g: (0, 0)),
            pl.BlockSpec((total, 2), lambda g: (0, 0)),
        ] + [pl.BlockSpec((sources, 1, slots, cols), lambda g: (0, g, 0, 0))] * halves,
        out_specs=pl.BlockSpec((places, 1, 4, cols), lambda g: (0, g, 0, 0)),
        out_shape=jax.ShapeDtypeStruct((places, bands, 4, cols), jnp.float32),
        scratch_shapes=[
            pltpu.VMEM((4, total, cols), jnp.bfloat16),
            pltpu.VMEM((4, places, cols), jnp.float32),
        ],
        name="compose",
    )(row, col, *got)


def exchange(parts):
    return lax.all_to_all(parts, AXES, split_axis=0, concat_axis=0, tiled=True)


def body(volume, resampler, ramp_slope, ramp_pivot, tile_owner, tile_cell, depth_order, slab_rank):
    brick_count, edge = volume.shape[:2]
    views, _, cols = resampler.shape
    slabs, tiles = lax.axis_size("depth"), lax.axis_size("tile")
    devices = slabs * tiles
    cells_each = CELLS // slabs
    base = slabs * devices * brick_count
    places = devices * cells_each
    halves = 2
    chunk = brick_count // halves
    bands, groups = max(1, edge // devices), max(1, devices // edge)

    rank = lax.dynamic_slice_in_dim(slab_rank, lax.axis_index("depth"), 1, 1)
    key = rank * (devices * brick_count) + depth_order
    owner, cell = tile_owner.T, tile_cell.T
    place = ((cell // cells_each) * tiles + owner) * cells_each + cell % cells_each
    code = place * base + key
    codes = exchange(jnp.broadcast_to(code.reshape(1, -1), (devices, views * brick_count)))
    codes = codes.reshape(devices, views, halves, chunk).transpose(1, 2, 0, 3).reshape(views, -1)
    floors = (codes // base) * base

    finals = []
    for view in range(views):
        got = []
        for half in range(halves):
            prints = render(volume, resampler[view], ramp_slope, ramp_pivot, view, half * chunk, chunk)
            prints = prints.reshape(edge, 4 * chunk, groups, cols // groups).transpose(0, 2, 1, 3)
            got.append(exchange(prints.reshape(devices, bands, 4 * chunk, cols // groups)))
        col = jnp.stack([codes[view], floors[view]], axis=1)
        made = compose(codes[view][None], col, got, places, base)
        final = exchange(made.reshape(devices, cells_each * bands * 4, cols // groups))
        final = final.reshape(edge // bands, groups, cells_each, bands, 4, cols // groups)
        finals.append(final.transpose(4, 2, 0, 3, 1, 5).reshape(4, cells_each * edge, cols))
    final = jnp.stack(finals)
    return final[:, :3, None], final[:, 3:]


def solution(mesh):
    in_specs = (
        P(AXES, None, None, None),
        P(),
        P(),
        P(),
        P(AXES, None),
        P(AXES, None),
        P(None, AXES),
        P(),
    )
    out_specs = (P(None, None, "tile", "depth", None), P(None, "tile", "depth", None))
    return jax.shard_map(body, mesh=mesh, in_specs=in_specs, out_specs=out_specs, check_vma=False)
```

```python
import functools

import jax
import jax.numpy as jnp
from jax import lax
from jax.experimental import pallas as pl
from jax.experimental.pallas import tpu as pltpu
from jax.sharding import PartitionSpec as P

LOG2E = 1.4426950408889634
GROUP = 16
STRIP = 16
CELLS = 8
TAGS = 8
AXES = ("depth", "tile")


def render_kernel(slope_ref, pivot_ref, code_ref, vol_ref, res_ref, out_ref, even_ref, odd_ref, ramp_ref, acc_ref, seen_ref, tint_ref, print_ref, *, view, count, tagged):
    step = pl.program_id(0)
    bricks = count
    edge = vol_ref.shape[1]
    cols = res_ref.shape[2]
    pitch = edge + 1
    blocks = edge // GROUP
    strip = STRIP
    rate = -LOG2E / edge

    def multiply(block, samp_ref):
        weights = res_ref[0]
        if view == 0:
            rows = vol_ref[0, pl.ds(block * GROUP, GROUP)].reshape(GROUP * edge, edge)
            made = jnp.dot(rows, weights, preferred_element_type=jnp.float32)
            samp_ref[pl.ds(block * GROUP * edge, GROUP * edge), :] = made
        else:
            for j in range(GROUP):
                made = lax.dot_general(
                    vol_ref[0, block * GROUP + j], weights, (((0,), (0,)), ((), ())),
                    preferred_element_type=jnp.float32)
                samp_ref[pl.ds(block * GROUP * pitch + j * pitch, edge), :] = made

    def start():
        acc_ref[...] = jnp.zeros_like(acc_ref)
        seen_ref[...] = jnp.ones_like(seen_ref)
        tint_ref[...] = jnp.zeros_like(tint_ref)

    def ramps():
        for ch in range(3):
            gain = jnp.full((16, cols), 0.5 * slope_ref[ch], jnp.float32)
            offset = -gain * pivot_ref[ch]
            for place, value in ((0, gain), (1, offset)):
                debt = jnp.zeros_like(value)
                for j in range(GROUP):
                    want = value + debt
                    given = want.astype(jnp.bfloat16)
                    debt = want - given.astype(jnp.float32)
                    ramp_ref[j, ch, place] = given

    def march(block, samp_ref):
        for top in range(0, edge, strip):
            acc = acc_ref[pl.ds(top, strip), :]
            seen = seen_ref[pl.ds(top, strip), :]
            part = [[] for _ in range(3)]
            for j in range(GROUP):
                if view == 0:
                    s = samp_ref[pl.ds((block * GROUP + j) * edge + top, strip), :]
                else:
                    s = samp_ref[pl.ds(top * pitch + block * GROUP + j, strip, stride=pitch), :]
                acc = acc + s
                left = jnp.exp2(acc * rate)
                w = (seen - left).astype(jnp.bfloat16)
                seen = left
                s16 = s.astype(jnp.bfloat16)
                for ch in range(3):
                    gain = jnp.concatenate([ramp_ref[j, ch, 0]] * (strip // 16), axis=0)
                    offset = jnp.concatenate([ramp_ref[j, ch, 1]] * (strip // 16), axis=0)
                    p = w * jnp.tanh(s16 * gain + offset)
                    n = j
                    while n % 2 == 1:
                        p = part[ch].pop() + p
                        n //= 2
                    part[ch].append(p)
            for ch in range(3):
                tint_ref[ch, pl.ds(top, strip), :] += part[ch][0].astype(jnp.float32)
            acc_ref[pl.ds(top, strip), :] = acc
            seen_ref[pl.ds(top, strip), :] = seen

    def finish(brick):
        alpha = 1.0 - seen_ref[...]
        for ch in range(3):
            print_ref[pl.ds((ch * bricks + brick) * pitch, edge), :] = 0.5 * (alpha + tint_ref[ch])
        print_ref[pl.ds((3 * bricks + brick) * pitch, edge), :] = acc_ref[...] * (1.0 / edge)

    def loop(f):
        def it(block, carry):
            f(block)
            return carry
        lax.fori_loop(0, blocks, it, 0)

    @pl.when(step == 0)
    def _():
        ramps()
        loop(lambda block: multiply(block, even_ref))

    for parity, (own, other) in enumerate(((even_ref, odd_ref), (odd_ref, even_ref))):
        @pl.when((step > 0) & (step < bricks) & (lax.rem(step, 2) == parity))
        def _():
            start()

            def both(block):
                multiply(block, own)
                march(block, other)
            loop(both)
            finish(step - 1)

    last = odd_ref if count % 2 == 0 else even_ref

    @pl.when(step == bricks)
    def _():
        start()
        loop(lambda block: march(block, last))
        finish(step - 1)

        if tagged:
            code = jnp.broadcast_to(code_ref[...], (TAGS, cols))
            digit = lax.broadcasted_iota(jnp.int32, (TAGS, cols), 0)
            tags = jnp.where(digit == 0, code & 255, jnp.where(digit == 1, (code >> 8) & 255, code >> 16)).astype(jnp.float32)

        def swap(row, carry):
            out_ref[row, :4 * bricks, :] = print_ref[pl.ds(row, 4 * bricks, stride=pitch), :].astype(jnp.bfloat16)
            if tagged:
                out_ref[row, 4 * bricks:, :] = tags.astype(jnp.bfloat16)
            return carry
        lax.fori_loop(0, edge, swap, 0, unroll=4)


def render(volume, resampler, slope, pivot, code, view, first, count, tagged):
    edge, cols = volume.shape[1], resampler.shape[2]
    pitch = edge + 1
    slots = 4 * count + (TAGS if tagged else 0)
    smem = pl.BlockSpec(memory_space=pltpu.SMEM)
    return pl.pallas_call(
        functools.partial(render_kernel, view=view, count=count, tagged=tagged),
        grid=(count + 1,),
        in_specs=[
            smem,
            smem,
            pl.BlockSpec((1, cols), lambda g: (0, 0)),
            pl.BlockSpec((1, edge, edge, edge), lambda g: (first + jnp.minimum(g, count - 1), 0, 0, 0)),
            pl.BlockSpec((1, edge, cols), lambda g: (view, 0, 0)),
        ],
        out_specs=pl.BlockSpec((edge, slots, cols), lambda g: (0, 0, 0)),
        out_shape=jax.ShapeDtypeStruct((edge, slots, cols), jnp.bfloat16),
        scratch_shapes=[
            pltpu.VMEM((edge * pitch, cols), jnp.float32),
            pltpu.VMEM((edge * pitch, cols), jnp.float32),
            pltpu.VMEM((GROUP, 3, 2, 16, cols), jnp.bfloat16),
            pltpu.VMEM((edge, cols), jnp.float32),
            pltpu.VMEM((edge, cols), jnp.float32),
            pltpu.VMEM((3, edge, cols), jnp.float32),
            pltpu.VMEM((4 * count * pitch, cols), jnp.float32),
        ],
        name=f"render{view}",
    )(slope, pivot, code, volume, resampler)


def compose_kernel(row_ref, col_ref, got_ref, *refs, base, count):
    out_ref, feat_ref, sum_ref = refs[-3:]
    total, cols = feat_ref.shape[1:]
    places = sum_ref.shape[1]
    for ch in range(4):
        part = got_ref[:, 0, ch * count:(ch + 1) * count, :].astype(jnp.float32)
        feat_ref[ch] = part.reshape(total, cols).astype(jnp.bfloat16)
    sum_ref[...] = jnp.zeros_like(sum_ref)
    block = min(256, total)
    row = row_ref[...]
    start = lax.broadcasted_iota(jnp.int32, (places, block), 0) * base

    def it(i, carry):
        rows = pl.ds(i * block, block)
        code = col_ref[rows, 0:1]
        floor = col_ref[rows, 1:2]
        before = ((row >= floor) & (row < code)).astype(jnp.float32).astype(jnp.bfloat16)
        inner = jnp.dot(before, feat_ref[3], preferred_element_type=jnp.float32)
        light = jnp.exp(-inner)
        own = row_ref[:, rows]
        pick = ((own >= start) & (own < start + base)).astype(jnp.float32).astype(jnp.bfloat16)
        for ch in range(4):
            value = feat_ref[ch, rows, :]
            if ch < 3:
                value = (value.astype(jnp.float32) * light).astype(jnp.bfloat16)
            sum_ref[ch] += jnp.dot(pick, value, preferred_element_type=jnp.float32)
        return carry

    lax.fori_loop(0, total // block, it, 0)
    for ch in range(3):
        out_ref[:, 0, 0, ch, :] = sum_ref[ch]
    out_ref[:, 0, 0, 3, :] = jnp.exp(-sum_ref[3])


def compose(row, col, got, made, view, views, count, places, base):
    sources, bands, slots, cols = got.shape
    total = row.shape[1]
    more = [] if made is None else [made]
    return pl.pallas_call(
        functools.partial(compose_kernel, base=base, count=count),
        grid=(bands,),
        in_specs=[
            pl.BlockSpec((1, total), lambda g: (0, 0)),
            pl.BlockSpec((total, 2), lambda g: (0, 0)),
            pl.BlockSpec((sources, 1, slots, cols), lambda g: (0, g, 0, 0)),
        ] + [pl.BlockSpec(memory_space=pl.ANY)] * len(more),
        out_specs=pl.BlockSpec((places, 1, 1, 4, cols), lambda g: (0, view, g, 0, 0)),
        out_shape=jax.ShapeDtypeStruct((places, views, bands, 4, cols), jnp.float32),
        scratch_shapes=[
            pltpu.VMEM((4, total, cols), jnp.bfloat16),
            pltpu.VMEM((4, places, cols), jnp.float32),
        ],
        input_output_aliases={3: 0} if more else {},
        name="compose",
    )(row, col, got, *more)


def exchange(parts):
    return lax.all_to_all(parts, AXES, split_axis=0, concat_axis=0, tiled=True)


def body(volume, resampler, ramp_slope, ramp_pivot, tile_owner, tile_cell, depth_order, slab_rank):
    count, edge = volume.shape[:2]
    views, _, cols = resampler.shape
    slabs, tiles = lax.axis_size("depth"), lax.axis_size("tile")
    devices = slabs * tiles
    cells_each = CELLS // slabs
    base = slabs * devices * count
    places = devices * cells_each
    bands, groups = max(1, edge // devices), max(1, devices // edge)
    width = cols // groups

    rank = lax.dynamic_slice_in_dim(slab_rank, lax.axis_index("depth"), 1, 1)
    key = rank * (devices * count) + depth_order
    owner, cell = tile_owner.T, tile_cell.T
    place = ((cell // cells_each) * tiles + owner) * cells_each + cell % cells_each
    code = (place * base + key).reshape(1, views * count)
    code = jnp.tile(code, (1, cols // (views * count)))

    order = list(range(views))[::-1]
    made, codes = None, None
    for view in order:
        tagged = view == order[0]
        prints = render(volume, resampler, ramp_slope, ramp_pivot, code, view, 0, count, tagged)
        prints = prints.reshape(edge, -1, groups, width).transpose(0, 2, 1, 3)
        got = exchange(prints.reshape(devices, bands, -1, width))
        if tagged:
            digits = got[:, 0, 4 * count:4 * count + 3, :views * count].astype(jnp.int32)
            codes = digits[:, 0] + digits[:, 1] * 256 + digits[:, 2] * 65536
            codes = codes.reshape(devices, views, count).transpose(1, 0, 2).reshape(views, -1)
            floors = (codes // base) * base
        col = jnp.stack([codes[view], floors[view]], axis=1)
        made = compose(codes[view][None], col, got, made, view, views, count, places, base)
    final = exchange(made.reshape(devices, cells_each * views * bands * 4, width))
    final = final.reshape(edge // bands, groups, cells_each, views, bands, 4, width)
    final = final.transpose(3, 5, 2, 0, 4, 1, 6).reshape(views, 4, cells_each * edge, cols)
    return final[:, :3, None], final[:, 3:]


def solution(mesh):
    in_specs = (
        P(AXES, None, None, None),
        P(),
        P(),
        P(),
        P(AXES, None),
        P(AXES, None),
        P(None, AXES),
        P(),
    )
    out_specs = (P(None, None, "tile", "depth", None), P(None, "tile", "depth", None))
    return jax.shard_map(body, mesh=mesh, in_specs=in_specs, out_specs=out_specs, check_vma=False)
```

```python
import functools

import jax
import jax.numpy as jnp
from jax import lax
from jax.experimental import pallas as pl
from jax.experimental.pallas import tpu as pltpu
from jax.sharding import PartitionSpec as P

LOG2E = 1.4426950408889634
GROUP = 16
STRIP = 16
CELLS = 8
TAGS = 8
AXES = ("depth", "tile")


def render_kernel(slope_ref, pivot_ref, code_ref, vol_ref, res_ref, out_ref, even_ref, odd_ref, ramp_ref, acc_ref, seen_ref, tint_ref, print_ref, *, view, count, tagged):
    step = pl.program_id(0)
    bricks = count
    edge = vol_ref.shape[1]
    cols = res_ref.shape[2]
    pitch = edge + 1
    blocks = edge // GROUP
    strip = STRIP
    rate = -LOG2E / edge

    def multiply(block, samp_ref):
        weights = res_ref[0]
        if view == 0:
            rows = vol_ref[0, pl.ds(block * GROUP, GROUP)].reshape(GROUP * edge, edge)
            made = jnp.dot(rows, weights, preferred_element_type=jnp.float32)
            samp_ref[pl.ds(block * GROUP * edge, GROUP * edge), :] = made
        else:
            for j in range(GROUP):
                made = lax.dot_general(
                    vol_ref[0, block * GROUP + j], weights, (((0,), (0,)), ((), ())),
                    preferred_element_type=jnp.float32)
                samp_ref[pl.ds(block * GROUP * pitch + j * pitch, edge), :] = made

    def start():
        acc_ref[...] = jnp.zeros_like(acc_ref)
        seen_ref[...] = jnp.ones_like(seen_ref)
        tint_ref[...] = jnp.zeros_like(tint_ref)

    def ramps():
        for ch in range(3):
            gain = jnp.full((16, cols), 0.5 * slope_ref[ch], jnp.float32)
            offset = -gain * pivot_ref[ch]
            for place, value in ((0, gain), (1, offset)):
                debt = jnp.zeros_like(value)
                for j in range(GROUP):
                    want = value + debt
                    given = want.astype(jnp.bfloat16)
                    debt = want - given.astype(jnp.float32)
                    ramp_ref[j, ch, place] = given

    def march(block, samp_ref):
        for top in range(0, edge, strip):
            acc = acc_ref[pl.ds(top, strip), :]
            seen = seen_ref[pl.ds(top, strip), :]
            part = [[] for _ in range(3)]
            for j in range(GROUP):
                if view == 0:
                    s = samp_ref[pl.ds((block * GROUP + j) * edge + top, strip), :]
                else:
                    s = samp_ref[pl.ds(top * pitch + block * GROUP + j, strip, stride=pitch), :]
                acc = acc + s
                left = jnp.exp2(acc * rate)
                w = (seen - left).astype(jnp.bfloat16)
                seen = left
                s16 = s.astype(jnp.bfloat16)
                for ch in range(3):
                    gain = jnp.concatenate([ramp_ref[j, ch, 0]] * (strip // 16), axis=0)
                    offset = jnp.concatenate([ramp_ref[j, ch, 1]] * (strip // 16), axis=0)
                    p = w * jnp.tanh(s16 * gain + offset)
                    n = j
                    while n % 2 == 1:
                        p = part[ch].pop() + p
                        n //= 2
                    part[ch].append(p)
            for ch in range(3):
                tint_ref[ch, pl.ds(top, strip), :] += part[ch][0].astype(jnp.float32)
            acc_ref[pl.ds(top, strip), :] = acc
            seen_ref[pl.ds(top, strip), :] = seen

    def finish(brick):
        alpha = 1.0 - seen_ref[...]
        for ch in range(3):
            print_ref[pl.ds((ch * bricks + brick) * pitch, edge), :] = 0.5 * (alpha + tint_ref[ch])
        print_ref[pl.ds((3 * bricks + brick) * pitch, edge), :] = acc_ref[...] * (1.0 / edge)

    def loop(f):
        def it(block, carry):
            f(block)
            return carry
        lax.fori_loop(0, blocks, it, 0)

    @pl.when(step == 0)
    def _():
        ramps()
        loop(lambda block: multiply(block, even_ref))

    for parity, (own, other) in enumerate(((even_ref, odd_ref), (odd_ref, even_ref))):
        @pl.when((step > 0) & (step < bricks) & (lax.rem(step, 2) == parity))
        def _():
            start()

            def both(block):
                multiply(block, own)
                march(block, other)
            loop(both)
            finish(step - 1)

    last = odd_ref if count % 2 == 0 else even_ref

    @pl.when(step == bricks)
    def _():
        start()
        loop(lambda block: march(block, last))
        finish(step - 1)

        if tagged:
            code = jnp.broadcast_to(code_ref[...], (TAGS, cols))
            digit = lax.broadcasted_iota(jnp.int32, (TAGS, cols), 0)
            tags = jnp.where(digit == 0, code & 255, jnp.where(digit == 1, (code >> 8) & 255, code >> 16)).astype(jnp.float32)

        def swap(row, carry):
            out_ref[row, :4 * bricks, :] = print_ref[pl.ds(row, 4 * bricks, stride=pitch), :].astype(jnp.bfloat16)
            if tagged:
                out_ref[row, 4 * bricks:, :] = tags.astype(jnp.bfloat16)
            return carry
        lax.fori_loop(0, edge, swap, 0, unroll=4)


def render(volume, resampler, slope, pivot, code, view, first, count, tagged):
    edge, cols = volume.shape[1], resampler.shape[2]
    pitch = edge + 1
    slots = 4 * count + (TAGS if tagged else 0)
    smem = pl.BlockSpec(memory_space=pltpu.SMEM)
    return pl.pallas_call(
        functools.partial(render_kernel, view=view, count=count, tagged=tagged),
        grid=(count + 1,),
        in_specs=[
            smem,
            smem,
            pl.BlockSpec((1, cols), lambda g: (0, 0)),
            pl.BlockSpec((1, edge, edge, edge), lambda g: (first + jnp.minimum(g, count - 1), 0, 0, 0)),
            pl.BlockSpec((1, edge, cols), lambda g: (view, 0, 0)),
        ],
        out_specs=pl.BlockSpec((edge, slots, cols), lambda g: (0, 0, 0)),
        out_shape=jax.ShapeDtypeStruct((edge, slots, cols), jnp.bfloat16),
        scratch_shapes=[
            pltpu.VMEM((edge * pitch, cols), jnp.float32),
            pltpu.VMEM((edge * pitch, cols), jnp.float32),
            pltpu.VMEM((GROUP, 3, 2, 16, cols), jnp.bfloat16),
            pltpu.VMEM((edge, cols), jnp.float32),
            pltpu.VMEM((edge, cols), jnp.float32),
            pltpu.VMEM((3, edge, cols), jnp.float32),
            pltpu.VMEM((4 * count * pitch, cols), jnp.float32),
        ],
        name=f"render{view}",
    )(slope, pivot, code, volume, resampler)


def compose_kernel(row_ref, col_ref, got_ref, *refs, base, count):
    out_ref, feat_ref, sum_ref, pack_ref = refs[-4:]
    total, lanes = feat_ref.shape[1:]
    places = sum_ref.shape[1]
    bands, width = got_ref.shape[1], got_ref.shape[3]
    for band in range(bands):
        for ch in range(4):
            part = got_ref[:, band, ch * count:(ch + 1) * count, :].astype(jnp.float32)
            feat_ref[ch, :, band * width:(band + 1) * width] = part.reshape(total, width).astype(jnp.bfloat16)
    sum_ref[...] = jnp.zeros_like(sum_ref)
    block = min(256, total)
    row = row_ref[...]
    start = lax.broadcasted_iota(jnp.int32, (places, block), 0) * base

    def it(i, carry):
        rows = pl.ds(i * block, block)
        code = col_ref[rows, 0:1]
        floor = col_ref[rows, 1:2]
        before = ((row >= floor) & (row < code)).astype(jnp.float32).astype(jnp.bfloat16)
        inner = jnp.dot(before, feat_ref[3], preferred_element_type=jnp.float32)
        light = jnp.exp(-inner)
        own = row_ref[:, rows]
        pick = ((own >= start) & (own < start + base)).astype(jnp.float32).astype(jnp.bfloat16)
        for ch in range(4):
            value = feat_ref[ch, rows, :]
            if ch < 3:
                value = (value.astype(jnp.float32) * light).astype(jnp.bfloat16)
            sum_ref[ch] += jnp.dot(pick, value, preferred_element_type=jnp.float32)
        return carry

    lax.fori_loop(0, total // block, it, 0)
    for band in range(bands):
        for ch in range(4):
            value = sum_ref[ch, :, band * width:(band + 1) * width]
            pack_ref[:, band * 4 + ch, :] = value if ch < 3 else jnp.exp(-value)
    out_ref[:, 0] = pack_ref[...].astype(jnp.bfloat16)


def compose(row, col, got, made, view, views, count, places, base):
    sources, bands, slots, width = got.shape
    total = row.shape[1]
    more = [] if made is None else [made]
    vmem = pl.BlockSpec(memory_space=pltpu.VMEM)
    return pl.pallas_call(
        functools.partial(compose_kernel, base=base, count=count),
        grid=(1,),
        in_specs=[vmem, vmem, vmem] + [pl.BlockSpec(memory_space=pl.ANY)] * len(more),
        out_specs=pl.BlockSpec((places, 1, bands * 4, width), lambda g: (0, view, 0, 0)),
        out_shape=jax.ShapeDtypeStruct((places, views, bands * 4, width), jnp.bfloat16),
        scratch_shapes=[
            pltpu.VMEM((4, total, bands * width), jnp.bfloat16),
            pltpu.VMEM((4, places, bands * width), jnp.float32),
            pltpu.VMEM((places, bands * 4, width), jnp.float32),
        ],
        input_output_aliases={3: 0} if more else {},
        name="compose",
    )(row, col, got, *more)


def exchange(parts):
    return lax.all_to_all(parts, AXES, split_axis=0, concat_axis=0, tiled=True)


def body(volume, resampler, ramp_slope, ramp_pivot, tile_owner, tile_cell, depth_order, slab_rank):
    count, edge = volume.shape[:2]
    views, _, cols = resampler.shape
    slabs, tiles = lax.axis_size("depth"), lax.axis_size("tile")
    devices = slabs * tiles
    cells_each = CELLS // slabs
    base = slabs * devices * count
    places = devices * cells_each
    bands, groups = max(1, edge // devices), max(1, devices // edge)
    width = cols // groups

    rank = lax.dynamic_slice_in_dim(slab_rank, lax.axis_index("depth"), 1, 1)
    key = rank * (devices * count) + depth_order
    owner, cell = tile_owner.T, tile_cell.T
    place = ((cell // cells_each) * tiles + owner) * cells_each + cell % cells_each
    code = (place * base + key).reshape(1, views * count)
    code = jnp.tile(code, (1, cols // (views * count)))

    order = list(range(views))[::-1]
    made, codes = None, None
    for view in order:
        tagged = view == order[0]
        prints = render(volume, resampler, ramp_slope, ramp_pivot, code, view, 0, count, tagged)
        prints = prints.reshape(edge, -1, groups, width).transpose(0, 2, 1, 3)
        got = exchange(prints.reshape(devices, bands, -1, width))
        if tagged:
            digits = got[:, 0, 4 * count:4 * count + 3, :views * count].astype(jnp.int32)
            codes = digits[:, 0] + digits[:, 1] * 256 + digits[:, 2] * 65536
            codes = codes.reshape(devices, views, count).transpose(1, 0, 2).reshape(views, -1)
            floors = (codes // base) * base
        col = jnp.stack([codes[view], floors[view]], axis=1)
        made = compose(codes[view][None], col, got, made, view, views, count, places, base)
    final = exchange(made.reshape(devices, cells_each * views, bands * 4, width))
    final = final.reshape(edge // bands, groups, cells_each, views, bands, 4, width)
    final = final.transpose(3, 5, 2, 0, 4, 1, 6).reshape(views, 4, cells_each * edge, cols)
    final = final.astype(jnp.float32)
    return final[:, :3, None], final[:, 3:]


def solution(mesh):
    in_specs = (
        P(AXES, None, None, None),
        P(),
        P(),
        P(),
        P(AXES, None),
        P(AXES, None),
        P(None, AXES),
        P(),
    )
    out_specs = (P(None, None, "tile", "depth", None), P(None, "tile", "depth", None))
    return jax.shard_map(body, mesh=mesh, in_specs=in_specs, out_specs=out_specs, check_vma=False)
```

```python
import functools

import jax
import jax.numpy as jnp
from jax import lax
from jax.experimental import pallas as pl
from jax.experimental.pallas import tpu as pltpu
from jax.sharding import PartitionSpec as P

LOG2E = 1.4426950408889634
GROUP = 16
STRIP = 16
CELLS = 8
TAGS = 8
AXES = ("depth", "tile")


def render_kernel(slope_ref, pivot_ref, code_ref, vol_ref, res_ref, out_ref, even_ref, odd_ref, ramp_ref, acc_ref, seen_ref, tint_ref, print_ref, *, view, count, tagged):
    step = pl.program_id(0)
    bricks = count
    edge = vol_ref.shape[1]
    cols = res_ref.shape[2]
    pitch = edge + 1
    blocks = edge // GROUP
    strip = STRIP
    rate = -LOG2E / edge

    def multiply(block, samp_ref):
        weights = res_ref[0]
        if view == 0:
            rows = vol_ref[0, pl.ds(block * GROUP, GROUP)].reshape(GROUP * edge, edge)
            made = jnp.dot(rows, weights, preferred_element_type=jnp.float32)
            samp_ref[pl.ds(block * GROUP * edge, GROUP * edge), :] = made
        else:
            for j in range(GROUP):
                made = lax.dot_general(
                    vol_ref[0, block * GROUP + j], weights, (((0,), (0,)), ((), ())),
                    preferred_element_type=jnp.float32)
                samp_ref[pl.ds(block * GROUP * pitch + j * pitch, edge), :] = made

    def start():
        acc_ref[...] = jnp.zeros_like(acc_ref)
        seen_ref[...] = jnp.ones_like(seen_ref)
        tint_ref[...] = jnp.zeros_like(tint_ref)

    def ramps():
        for ch in range(3):
            gain = jnp.full((16, cols), 0.5 * slope_ref[ch], jnp.float32)
            offset = -gain * pivot_ref[ch]
            for place, value in ((0, gain), (1, offset)):
                debt = jnp.zeros_like(value)
                for j in range(GROUP):
                    want = value + debt
                    given = want.astype(jnp.bfloat16)
                    debt = want - given.astype(jnp.float32)
                    ramp_ref[j, ch, place] = given

    def march(block, samp_ref):
        for top in range(0, edge, strip):
            acc = acc_ref[pl.ds(top, strip), :]
            seen = seen_ref[pl.ds(top, strip), :]
            part = [[] for _ in range(3)]
            for j in range(GROUP):
                if view == 0:
                    s = samp_ref[pl.ds((block * GROUP + j) * edge + top, strip), :]
                else:
                    s = samp_ref[pl.ds(top * pitch + block * GROUP + j, strip, stride=pitch), :]
                acc = acc + s
                left = jnp.exp2(acc * rate)
                w = (seen - left).astype(jnp.bfloat16)
                seen = left
                s16 = s.astype(jnp.bfloat16)
                for ch in range(3):
                    gain = jnp.concatenate([ramp_ref[j, ch, 0]] * (strip // 16), axis=0)
                    offset = jnp.concatenate([ramp_ref[j, ch, 1]] * (strip // 16), axis=0)
                    p = w * jnp.tanh(s16 * gain + offset)
                    n = j
                    while n % 2 == 1:
                        p = part[ch].pop() + p
                        n //= 2
                    part[ch].append(p)
            for ch in range(3):
                tint_ref[ch, pl.ds(top, strip), :] += part[ch][0].astype(jnp.float32)
            acc_ref[pl.ds(top, strip), :] = acc
            seen_ref[pl.ds(top, strip), :] = seen

    def finish(brick):
        alpha = 1.0 - seen_ref[...]
        for ch in range(3):
            print_ref[pl.ds((ch * bricks + brick) * pitch, edge), :] = 0.5 * (alpha + tint_ref[ch])
        print_ref[pl.ds((3 * bricks + brick) * pitch, edge), :] = acc_ref[...] * (1.0 / edge)

    def loop(f):
        def it(block, carry):
            f(block)
            return carry
        lax.fori_loop(0, blocks, it, 0)

    @pl.when(step == 0)
    def _():
        ramps()
        loop(lambda block: multiply(block, even_ref))

    for parity, (own, other) in enumerate(((even_ref, odd_ref), (odd_ref, even_ref))):
        @pl.when((step > 0) & (step < bricks) & (lax.rem(step, 2) == parity))
        def _():
            start()

            def both(block):
                multiply(block, own)
                march(block, other)
            loop(both)
            finish(step - 1)

    last = odd_ref if count % 2 == 0 else even_ref

    @pl.when(step == bricks)
    def _():
        start()
        loop(lambda block: march(block, last))
        finish(step - 1)

        if tagged:
            code = jnp.broadcast_to(code_ref[...], (TAGS, cols))
            digit = lax.broadcasted_iota(jnp.int32, (TAGS, cols), 0)
            tags = jnp.where(digit == 0, code & 255, jnp.where(digit == 1, (code >> 8) & 255, code >> 16)).astype(jnp.float32)

        def swap(row, carry):
            out_ref[row, :4 * bricks, :] = print_ref[pl.ds(row, 4 * bricks, stride=pitch), :].astype(jnp.bfloat16)
            if tagged:
                out_ref[row, 4 * bricks:, :] = tags.astype(jnp.bfloat16)
            return carry
        lax.fori_loop(0, edge, swap, 0, unroll=4)


def render(volume, resampler, slope, pivot, code, view, first, count, tagged):
    edge, cols = volume.shape[1], resampler.shape[2]
    pitch = edge + 1
    slots = 4 * count + (TAGS if tagged else 0)
    smem = pl.BlockSpec(memory_space=pltpu.SMEM)
    return pl.pallas_call(
        functools.partial(render_kernel, view=view, count=count, tagged=tagged),
        grid=(count + 1,),
        in_specs=[
            smem,
            smem,
            pl.BlockSpec((1, cols), lambda g: (0, 0)),
            pl.BlockSpec((1, edge, edge, edge), lambda g: (first + jnp.minimum(g, count - 1), 0, 0, 0)),
            pl.BlockSpec((1, edge, cols), lambda g: (view, 0, 0)),
        ],
        out_specs=pl.BlockSpec((edge, slots, cols), lambda g: (0, 0, 0)),
        out_shape=jax.ShapeDtypeStruct((edge, slots, cols), jnp.bfloat16),
        scratch_shapes=[
            pltpu.VMEM((edge * pitch, cols), jnp.float32),
            pltpu.VMEM((edge * pitch, cols), jnp.float32),
            pltpu.VMEM((GROUP, 3, 2, 16, cols), jnp.bfloat16),
            pltpu.VMEM((edge, cols), jnp.float32),
            pltpu.VMEM((edge, cols), jnp.float32),
            pltpu.VMEM((3, edge, cols), jnp.float32),
            pltpu.VMEM((4 * count * pitch, cols), jnp.float32),
        ],
        name=f"render{view}",
    )(slope, pivot, code, volume, resampler)


def compose_kernel(row_ref, col_ref, got_ref, *refs, base, count):
    out_ref, feat_ref, sum_ref, pack_ref = refs[-4:]
    total, lanes = feat_ref.shape[1:]
    places = sum_ref.shape[1]
    bands, width = got_ref.shape[1], got_ref.shape[3]
    for band in range(bands):
        for ch in range(4):
            part = got_ref[:, band, ch * count:(ch + 1) * count, :].astype(jnp.float32)
            feat_ref[ch, :, band * width:(band + 1) * width] = part.reshape(total, width).astype(jnp.bfloat16)
    sum_ref[...] = jnp.zeros_like(sum_ref)
    block = min(256, total)
    row = row_ref[...]
    start = lax.broadcasted_iota(jnp.int32, (places, block), 0) * base

    def it(i, carry):
        rows = pl.ds(i * block, block)
        code = col_ref[rows, 0:1]
        floor = col_ref[rows, 1:2]
        before = ((row >= floor) & (row < code)).astype(jnp.float32).astype(jnp.bfloat16)
        inner = jnp.dot(before, feat_ref[3], preferred_element_type=jnp.float32)
        light = jnp.exp(-inner)
        own = row_ref[:, rows]
        pick = ((own >= start) & (own < start + base)).astype(jnp.float32).astype(jnp.bfloat16)
        for ch in range(4):
            value = feat_ref[ch, rows, :]
            if ch < 3:
                value = (value.astype(jnp.float32) * light).astype(jnp.bfloat16)
            sum_ref[ch] += jnp.dot(pick, value, preferred_element_type=jnp.float32)
        return carry

    lax.fori_loop(0, total // block, it, 0)
    for band in range(bands):
        for ch in range(4):
            value = sum_ref[ch, :, band * width:(band + 1) * width]
            pack_ref[:, band * 4 + ch, :] = value if ch < 3 else jnp.exp(-0.5 * value)
    out_ref[:, 0] = pack_ref[...].astype(out_ref.dtype)


def compose(row, col, got, made, view, views, count, places, base):
    sources, bands, slots, width = got.shape
    total = row.shape[1]
    more = [] if made is None else [made]
    vmem = pl.BlockSpec(memory_space=pltpu.VMEM)
    return pl.pallas_call(
        functools.partial(compose_kernel, base=base, count=count),
        grid=(1,),
        in_specs=[vmem, vmem, vmem] + [pl.BlockSpec(memory_space=pl.ANY)] * len(more),
        out_specs=pl.BlockSpec((places, 1, bands * 4, width), lambda g: (0, view, 0, 0)),
        out_shape=jax.ShapeDtypeStruct((places, views, bands * 4, width), jnp.float32),
        scratch_shapes=[
            pltpu.VMEM((4, total, bands * width), jnp.bfloat16),
            pltpu.VMEM((4, places, bands * width), jnp.float32),
            pltpu.VMEM((places, bands * 4, width), jnp.float32),
        ],
        input_output_aliases={3: 0} if more else {},
        name="compose",
    )(row, col, got, *more)


def exchange(parts):
    return lax.all_to_all(parts, AXES, split_axis=0, concat_axis=0, tiled=True)


def body(volume, resampler, ramp_slope, ramp_pivot, tile_owner, tile_cell, depth_order, slab_rank):
    count, edge = volume.shape[:2]
    views, _, cols = resampler.shape
    slabs, tiles = lax.axis_size("depth"), lax.axis_size("tile")
    devices = slabs * tiles
    cells_each = CELLS // slabs
    base = slabs * devices * count
    places = devices * cells_each
    bands, groups = max(1, edge // devices), max(1, devices // edge)
    width = cols // groups

    rank = lax.dynamic_slice_in_dim(slab_rank, lax.axis_index("depth"), 1, 1)
    key = rank * (devices * count) + depth_order
    owner, cell = tile_owner.T, tile_cell.T
    place = ((cell // cells_each) * tiles + owner) * cells_each + cell % cells_each
    code = (place * base + key).reshape(1, views * count)
    code = jnp.tile(code, (1, cols // (views * count)))

    order = list(range(views))[::-1]
    made, codes = None, None
    for view in order:
        tagged = view == order[0]
        prints = render(volume, resampler, ramp_slope, ramp_pivot, code, view, 0, count, tagged)
        prints = prints.reshape(edge, -1, groups, width).transpose(0, 2, 1, 3)
        got = exchange(prints.reshape(devices, bands, -1, width))
        if tagged:
            digits = got[:, 0, 4 * count:4 * count + 3, :views * count].astype(jnp.int32)
            codes = digits[:, 0] + digits[:, 1] * 256 + digits[:, 2] * 65536
            codes = codes.reshape(devices, views, count).transpose(1, 0, 2).reshape(views, -1)
            floors = (codes // base) * base
        col = jnp.stack([codes[view], floors[view]], axis=1)
        made = compose(codes[view][None], col, got, made, view, views, count, places, base)
    final = exchange(made.astype(jnp.float16).reshape(devices, cells_each * views, bands * 4, width))
    final = final.reshape(edge // bands, groups, cells_each, views, bands, 4, width)
    final = final.transpose(3, 5, 2, 0, 4, 1, 6).reshape(views, 4, cells_each * edge, cols)
    final = final.astype(jnp.float32)
    return final[:, :3, None], jnp.square(final[:, 3:])


def solution(mesh):
    in_specs = (
        P(AXES, None, None, None),
        P(),
        P(),
        P(),
        P(AXES, None),
        P(AXES, None),
        P(None, AXES),
        P(),
    )
    out_specs = (P(None, None, "tile", "depth", None), P(None, "tile", "depth", None))
    return jax.shard_map(body, mesh=mesh, in_specs=in_specs, out_specs=out_specs, check_vma=False)
```

```python
import functools

import jax
import jax.numpy as jnp
from jax import lax
from jax.experimental import pallas as pl
from jax.experimental.pallas import tpu as pltpu
from jax.sharding import PartitionSpec as P

LOG2E = 1.4426950408889634
GROUP = 16
STRIP = 16
CELLS = 8
TAGS = 8
AXES = ("depth", "tile")


def render_kernel(slope_ref, pivot_ref, owner_ref, cell_ref, order_ref, rank_ref, slab_ref, vol_ref, res_ref, out_ref, even_ref, odd_ref, ramp_ref, acc_ref, seen_ref, tint_ref, print_ref, *, view, count, tagged, tiles):
    step = pl.program_id(0)
    bricks = count
    edge = vol_ref.shape[1]
    cols = res_ref.shape[2]
    pitch = edge + 1
    blocks = edge // GROUP
    strip = STRIP
    rate = -LOG2E / edge

    def multiply(block, samp_ref):
        weights = res_ref[0]
        if view == 0:
            rows = vol_ref[0, pl.ds(block * GROUP, GROUP)].reshape(GROUP * edge, edge)
            made = jnp.dot(rows, weights, preferred_element_type=jnp.float32)
            samp_ref[pl.ds(block * GROUP * edge, GROUP * edge), :] = made
        else:
            for j in range(GROUP):
                made = lax.dot_general(
                    vol_ref[0, block * GROUP + j], weights, (((0,), (0,)), ((), ())),
                    preferred_element_type=jnp.float32)
                samp_ref[pl.ds(block * GROUP * pitch + j * pitch, edge), :] = made

    def start():
        acc_ref[...] = jnp.zeros_like(acc_ref)
        seen_ref[...] = jnp.ones_like(seen_ref)
        tint_ref[...] = jnp.zeros_like(tint_ref)

    def ramps():
        for ch in range(3):
            gain = jnp.full((16, cols), 0.5 * slope_ref[ch], jnp.float32)
            offset = -gain * pivot_ref[ch]
            for place, value in ((0, gain), (1, offset)):
                debt = jnp.zeros_like(value)
                for j in range(GROUP):
                    want = value + debt
                    given = want.astype(jnp.bfloat16)
                    debt = want - given.astype(jnp.float32)
                    ramp_ref[j, ch, place] = given

    def march(block, samp_ref):
        for top in range(0, edge, strip):
            acc = acc_ref[pl.ds(top, strip), :]
            seen = seen_ref[pl.ds(top, strip), :]
            part = [[] for _ in range(3)]
            for j in range(GROUP):
                if view == 0:
                    s = samp_ref[pl.ds((block * GROUP + j) * edge + top, strip), :]
                else:
                    s = samp_ref[pl.ds(top * pitch + block * GROUP + j, strip, stride=pitch), :]
                acc = acc + s
                left = jnp.exp2(acc * rate)
                w = (seen - left).astype(jnp.bfloat16)
                seen = left
                s16 = s.astype(jnp.bfloat16)
                for ch in range(3):
                    gain = jnp.concatenate([ramp_ref[j, ch, 0]] * (strip // 16), axis=0)
                    offset = jnp.concatenate([ramp_ref[j, ch, 1]] * (strip // 16), axis=0)
                    p = w * jnp.tanh(s16 * gain + offset)
                    n = j
                    while n % 2 == 1:
                        p = part[ch].pop() + p
                        n //= 2
                    part[ch].append(p)
            for ch in range(3):
                tint_ref[ch, pl.ds(top, strip), :] += part[ch][0].astype(jnp.float32)
            acc_ref[pl.ds(top, strip), :] = acc
            seen_ref[pl.ds(top, strip), :] = seen

    def finish(brick):
        alpha = 1.0 - seen_ref[...]
        for ch in range(3):
            print_ref[pl.ds((ch * bricks + brick) * pitch, edge), :] = 0.5 * (alpha + tint_ref[ch])
        print_ref[pl.ds((3 * bricks + brick) * pitch, edge), :] = acc_ref[...] * (1.0 / edge)

    def loop(f):
        def it(block, carry):
            f(block)
            return carry
        lax.fori_loop(0, blocks, it, 0)

    @pl.when(step == 0)
    def _():
        ramps()
        loop(lambda block: multiply(block, even_ref))

    for parity, (own, other) in enumerate(((even_ref, odd_ref), (odd_ref, even_ref))):
        @pl.when((step > 0) & (step < bricks) & (lax.rem(step, 2) == parity))
        def _():
            start()

            def both(block):
                multiply(block, own)
                march(block, other)
            loop(both)
            finish(step - 1)

    last = odd_ref if count % 2 == 0 else even_ref

    @pl.when(step == bricks)
    def _():
        start()
        loop(lambda block: march(block, last))
        finish(step - 1)

        if tagged:
            views = order_ref.shape[0]
            slabs = rank_ref.shape[1]
            cells_each = CELLS // slabs
            bricks_all = slabs * tiles * count
            lane = lax.rem(lax.broadcasted_iota(jnp.int32, (TAGS, cols), 1), views * count)
            code = jnp.zeros((TAGS, cols), jnp.int32)
            for v in range(views):
                rank = rank_ref[v, slab_ref[0]]
                for b in range(count):
                    cell = cell_ref[b, v]
                    group = lax.div(cell, cells_each)
                    place = (group * tiles + owner_ref[b, v]) * cells_each + (cell - group * cells_each)
                    value = (place * slabs + rank) * bricks_all + order_ref[v, b]
                    code = jnp.where(lane == v * count + b, value, code)
            digit = lax.broadcasted_iota(jnp.int32, (TAGS, cols), 0)
            tags = jnp.where(digit == 0, code & 255, jnp.where(digit == 1, (code >> 8) & 255, code >> 16)).astype(jnp.float32)

        def swap(row, carry):
            out_ref[row, :4 * bricks, :] = print_ref[pl.ds(row, 4 * bricks, stride=pitch), :].astype(jnp.bfloat16)
            if tagged:
                out_ref[row, 4 * bricks:, :] = tags.astype(jnp.bfloat16)
            return carry
        lax.fori_loop(0, edge, swap, 0, unroll=4)


def render(volume, resampler, slope, pivot, tags, view, first, count, tagged):
    edge, cols = volume.shape[1], resampler.shape[2]
    pitch = edge + 1
    slots = 4 * count + (TAGS if tagged else 0)
    smem = pl.BlockSpec(memory_space=pltpu.SMEM)
    return pl.pallas_call(
        functools.partial(render_kernel, view=view, count=count, tagged=tagged, tiles=lax.axis_size("tile")),
        grid=(count + 1,),
        in_specs=[
            smem,
            smem,
        ] + [smem] * len(tags) + [
            pl.BlockSpec((1, edge, edge, edge), lambda g: (first + jnp.minimum(g, count - 1), 0, 0, 0)),
            pl.BlockSpec((1, edge, cols), lambda g: (view, 0, 0)),
        ],
        out_specs=pl.BlockSpec((edge, slots, cols), lambda g: (0, 0, 0)),
        out_shape=jax.ShapeDtypeStruct((edge, slots, cols), jnp.bfloat16),
        scratch_shapes=[
            pltpu.VMEM((edge * pitch, cols), jnp.float32),
            pltpu.VMEM((edge * pitch, cols), jnp.float32),
            pltpu.VMEM((GROUP, 3, 2, 16, cols), jnp.bfloat16),
            pltpu.VMEM((edge, cols), jnp.float32),
            pltpu.VMEM((edge, cols), jnp.float32),
            pltpu.VMEM((3, edge, cols), jnp.float32),
            pltpu.VMEM((4 * count * pitch, cols), jnp.float32),
        ],
        name=f"render{view}",
    )(slope, pivot, *tags, volume, resampler)


def compose_kernel(row_ref, col_ref, got_ref, *refs, base, count):
    out_ref, feat_ref, sum_ref, pack_ref = refs[-4:]
    total, lanes = feat_ref.shape[1:]
    places = sum_ref.shape[1]
    bands, width = got_ref.shape[1], got_ref.shape[3]
    for band in range(bands):
        for ch in range(4):
            part = got_ref[:, band, ch * count:(ch + 1) * count, :]
            feat_ref[ch, :, band * width:(band + 1) * width] = part.reshape(total, width)
    sum_ref[...] = jnp.zeros_like(sum_ref)
    block = min(256, total)
    row = row_ref[...]
    start = lax.broadcasted_iota(jnp.int32, (places, block), 0) * base

    def it(i, carry):
        rows = pl.ds(i * block, block)
        code = col_ref[rows, 0:1]
        floor = col_ref[rows, 1:2]
        before = ((row >= floor) & (row < code)).astype(jnp.float32).astype(jnp.bfloat16)
        inner = jnp.dot(before, feat_ref[3], preferred_element_type=jnp.float32)
        light = jnp.exp(-inner)
        own = row_ref[:, rows]
        pick = ((own >= start) & (own < start + base)).astype(jnp.float32).astype(jnp.bfloat16)
        for ch in range(4):
            value = feat_ref[ch, rows, :]
            if ch < 3:
                value = (value.astype(jnp.float32) * light).astype(jnp.bfloat16)
            sum_ref[ch] += jnp.dot(pick, value, preferred_element_type=jnp.float32)
        return carry

    lax.fori_loop(0, total // block, it, 0)
    for band in range(bands):
        for ch in range(4):
            value = sum_ref[ch, :, band * width:(band + 1) * width]
            pack_ref[:, band * 4 + ch, :] = value if ch < 3 else jnp.exp(-0.5 * value)
    out_ref[:, 0] = pack_ref[...].astype(out_ref.dtype)


def compose(row, col, got, made, view, views, count, places, base):
    sources, bands, slots, width = got.shape
    total = row.shape[1]
    more = [] if made is None else [made]
    vmem = pl.BlockSpec(memory_space=pltpu.VMEM)
    return pl.pallas_call(
        functools.partial(compose_kernel, base=base, count=count),
        grid=(1,),
        in_specs=[vmem, vmem, vmem] + [pl.BlockSpec(memory_space=pl.ANY)] * len(more),
        out_specs=pl.BlockSpec((places, 1, bands * 4, width), lambda g: (0, view, 0, 0)),
        out_shape=jax.ShapeDtypeStruct((places, views, bands * 4, width), jnp.float32),
        scratch_shapes=[
            pltpu.VMEM((4, total, bands * width), jnp.bfloat16),
            pltpu.VMEM((4, places, bands * width), jnp.float32),
            pltpu.VMEM((places, bands * 4, width), jnp.float32),
        ],
        input_output_aliases={3: 0} if more else {},
        compiler_params=pltpu.CompilerParams(vmem_limit_bytes=32 << 20),
        name="compose",
    )(row, col, got, *more)


def exchange(parts):
    return lax.all_to_all(parts, AXES, split_axis=0, concat_axis=0, tiled=True)


def body(volume, resampler, ramp_slope, ramp_pivot, tile_owner, tile_cell, depth_order, slab_rank):
    count, edge = volume.shape[:2]
    views, _, cols = resampler.shape
    slabs, tiles = lax.axis_size("depth"), lax.axis_size("tile")
    devices = slabs * tiles
    cells_each = CELLS // slabs
    base = slabs * devices * count
    places = devices * cells_each
    bands, groups = max(1, edge // devices), max(1, devices // edge)
    width = cols // groups

    slab = lax.axis_index("depth").astype(jnp.int32).reshape(1)
    tags = (tile_owner, tile_cell, depth_order, slab_rank, slab)

    order = list(range(views))[::-1]
    made, codes = None, None
    for view in order:
        tagged = view == order[0]
        prints = render(volume, resampler, ramp_slope, ramp_pivot, tags, view, 0, count, tagged)
        prints = prints.reshape(edge, -1, groups, width).transpose(0, 2, 1, 3)
        got = exchange(prints.reshape(devices, bands, -1, width))
        if tagged:
            digits = got[:, 0, 4 * count:4 * count + 3, :views * count].astype(jnp.int32)
            codes = digits[:, 0] + digits[:, 1] * 256 + digits[:, 2] * 65536
            codes = codes.reshape(devices, views, count).transpose(1, 0, 2).reshape(views, -1)
            floors = (codes // base) * base
        col = jnp.stack([codes[view], floors[view]], axis=1)
        made = compose(codes[view][None], col, got, made, view, views, count, places, base)
    final = exchange(made.astype(jnp.float16).reshape(devices, cells_each * views, bands * 4, width))
    final = final.reshape(edge // bands, groups, cells_each, views, bands, 4, width)
    final = final.transpose(3, 5, 2, 0, 4, 1, 6).reshape(views, 4, cells_each * edge, cols)
    final = final.astype(jnp.float32)
    return final[:, :3, None], jnp.square(final[:, 3:])


def solution(mesh):
    in_specs = (
        P(AXES, None, None, None),
        P(),
        P(),
        P(),
        P(AXES, None),
        P(AXES, None),
        P(None, AXES),
        P(),
    )
    out_specs = (P(None, None, "tile", "depth", None), P(None, "tile", "depth", None))
    return jax.shard_map(body, mesh=mesh, in_specs=in_specs, out_specs=out_specs, check_vma=False)
```

```python
import functools

import jax
import jax.numpy as jnp
from jax import lax
from jax.experimental import pallas as pl
from jax.experimental.pallas import tpu as pltpu
from jax.sharding import PartitionSpec as P

LOG2E = 1.4426950408889634
GROUP = 16
STRIP = 16
CELLS = 8
TAGS = 8
AXES = ("depth", "tile")


def render_kernel(slope_ref, pivot_ref, owner_ref, cell_ref, order_ref, rank_ref, slab_ref, vol_ref, res_ref, out_ref, even_ref, odd_ref, ramp_ref, acc_ref, seen_ref, tint_ref, print_ref, *, view, count, tagged, tiles, bands):
    step = pl.program_id(0)
    bricks = count
    edge = vol_ref.shape[1]
    cols = res_ref.shape[2]
    pitch = edge + 1
    blocks = edge // GROUP
    strip = STRIP
    rate = -LOG2E / edge

    def multiply(block, samp_ref):
        weights = res_ref[0]
        if view == 0:
            rows = vol_ref[0, pl.ds(block * GROUP, GROUP)].reshape(GROUP * edge, edge)
            made = jnp.dot(rows, weights, preferred_element_type=jnp.float32)
            samp_ref[pl.ds(block * GROUP * edge, GROUP * edge), :] = made
        else:
            for j in range(GROUP):
                made = lax.dot_general(
                    vol_ref[0, block * GROUP + j], weights, (((0,), (0,)), ((), ())),
                    preferred_element_type=jnp.float32)
                samp_ref[pl.ds(block * GROUP * pitch + j * pitch, edge), :] = made

    def start():
        acc_ref[...] = jnp.zeros_like(acc_ref)
        seen_ref[...] = jnp.ones_like(seen_ref)
        tint_ref[...] = jnp.zeros_like(tint_ref)

    def ramps():
        for ch in range(3):
            gain = jnp.full((16, cols), 0.5 * slope_ref[ch], jnp.float32)
            offset = -gain * pivot_ref[ch]
            for place, value in ((0, gain), (1, offset)):
                debt = jnp.zeros_like(value)
                for j in range(GROUP):
                    want = value + debt
                    given = want.astype(jnp.bfloat16)
                    debt = want - given.astype(jnp.float32)
                    ramp_ref[j, ch, place] = given

    def march(block, samp_ref):
        for top in range(0, edge, strip):
            acc = acc_ref[pl.ds(top, strip), :]
            seen = seen_ref[pl.ds(top, strip), :]
            part = [[] for _ in range(3)]
            for j in range(GROUP):
                if view == 0:
                    s = samp_ref[pl.ds((block * GROUP + j) * edge + top, strip), :]
                else:
                    s = samp_ref[pl.ds(top * pitch + block * GROUP + j, strip, stride=pitch), :]
                acc = acc + s
                left = jnp.exp2(acc * rate)
                w = (seen - left).astype(jnp.bfloat16)
                seen = left
                s16 = s.astype(jnp.bfloat16)
                for ch in range(3):
                    gain = jnp.concatenate([ramp_ref[j, ch, 0]] * (strip // 16), axis=0)
                    offset = jnp.concatenate([ramp_ref[j, ch, 1]] * (strip // 16), axis=0)
                    p = w * jnp.tanh(s16 * gain + offset)
                    n = j
                    while n % 2 == 1:
                        p = part[ch].pop() + p
                        n //= 2
                    part[ch].append(p)
            for ch in range(3):
                tint_ref[ch, pl.ds(top, strip), :] += part[ch][0].astype(jnp.float32)
            acc_ref[pl.ds(top, strip), :] = acc
            seen_ref[pl.ds(top, strip), :] = seen

    def finish(brick):
        alpha = 1.0 - seen_ref[...]
        for ch in range(3):
            print_ref[pl.ds((ch * bricks + brick) * pitch, edge), :] = 0.5 * (alpha + tint_ref[ch])
        print_ref[pl.ds((3 * bricks + brick) * pitch, edge), :] = acc_ref[...] * (1.0 / edge)

    def loop(f):
        def it(block, carry):
            f(block)
            return carry
        lax.fori_loop(0, blocks, it, 0)

    @pl.when(step == 0)
    def _():
        ramps()
        loop(lambda block: multiply(block, even_ref))

    for parity, (own, other) in enumerate(((even_ref, odd_ref), (odd_ref, even_ref))):
        @pl.when((step > 0) & (step < bricks) & (lax.rem(step, 2) == parity))
        def _():
            start()

            def both(block):
                multiply(block, own)
                march(block, other)
            loop(both)
            finish(step - 1)

    last = odd_ref if count % 2 == 0 else even_ref

    @pl.when(step == bricks)
    def _():
        start()
        loop(lambda block: march(block, last))
        finish(step - 1)

        if tagged:
            views = order_ref.shape[0]
            slabs = rank_ref.shape[1]
            cells_each = CELLS // slabs
            bricks_all = slabs * tiles * count
            lane = lax.rem(lax.broadcasted_iota(jnp.int32, (TAGS, cols), 1), views * count)
            code = jnp.zeros((TAGS, cols), jnp.int32)
            for v in range(views):
                rank = rank_ref[v, slab_ref[0]]
                for b in range(count):
                    cell = cell_ref[v, b]
                    group = lax.div(cell, cells_each)
                    place = (group * tiles + owner_ref[v, b]) * cells_each + (cell - group * cells_each)
                    value = (place * slabs + rank) * bricks_all + order_ref[v, b]
                    code = jnp.where(lane == v * count + b, value, code)
            digit = lax.broadcasted_iota(jnp.int32, (TAGS, cols), 0)
            tags = jnp.where(digit == 0, code & 255, jnp.where(digit == 1, (code >> 8) & 255, code >> 16)).astype(jnp.float32)

        def swap(row, carry):
            for band in range(bands):
                part = print_ref[pl.ds(row * bands + band, 4 * bricks, stride=pitch), :]
                out_ref[row, band * 4 * bricks:(band + 1) * 4 * bricks, :] = part.astype(jnp.bfloat16)
            if tagged:
                out_ref[row, bands * 4 * bricks:, :] = tags.astype(jnp.bfloat16)
            return carry
        lax.fori_loop(0, edge // bands, swap, 0, unroll=2)


def render(volume, resampler, slope, pivot, tags, view, first, count, bands, tagged):
    edge, cols = volume.shape[1], resampler.shape[2]
    pitch = edge + 1
    slots = bands * 4 * count + (TAGS if tagged else 0)
    smem = pl.BlockSpec(memory_space=pltpu.SMEM)
    return pl.pallas_call(
        functools.partial(render_kernel, view=view, count=count, tagged=tagged, tiles=lax.axis_size("tile"), bands=bands),
        grid=(count + 1,),
        in_specs=[
            smem,
            smem,
        ] + [smem] * len(tags) + [
            pl.BlockSpec((1, edge, edge, edge), lambda g: (first + jnp.minimum(g, count - 1), 0, 0, 0)),
            pl.BlockSpec((1, edge, cols), lambda g: (view, 0, 0)),
        ],
        out_specs=pl.BlockSpec((edge // bands, slots, cols), lambda g: (0, 0, 0)),
        out_shape=jax.ShapeDtypeStruct((edge // bands, slots, cols), jnp.bfloat16),
        scratch_shapes=[
            pltpu.VMEM((edge * pitch, cols), jnp.float32),
            pltpu.VMEM((edge * pitch, cols), jnp.float32),
            pltpu.VMEM((GROUP, 3, 2, 16, cols), jnp.bfloat16),
            pltpu.VMEM((edge, cols), jnp.float32),
            pltpu.VMEM((edge, cols), jnp.float32),
            pltpu.VMEM((3, edge, cols), jnp.float32),
            pltpu.VMEM((4 * count * pitch, cols), jnp.float32),
        ],
        name=f"render{view}",
    )(slope, pivot, *tags, volume, resampler)


def compose_kernel(row_ref, col_ref, got_ref, *refs, base, count):
    out_ref, feat_ref, sum_ref, pack_ref = refs[-4:]
    total, lanes = feat_ref.shape[1:]
    places = sum_ref.shape[1]
    width = got_ref.shape[2]
    bands = lanes // width
    for band in range(bands):
        for ch in range(4):
            first = (band * 4 + ch) * count
            part = got_ref[:, first:first + count, :]
            feat_ref[ch, :, band * width:(band + 1) * width] = part.reshape(total, width)
    sum_ref[...] = jnp.zeros_like(sum_ref)
    block = min(256, total)
    row = row_ref[...]
    start = lax.broadcasted_iota(jnp.int32, (places, block), 0) * base

    def it(i, carry):
        rows = pl.ds(i * block, block)
        code = col_ref[rows, 0:1]
        floor = col_ref[rows, 1:2]
        before = ((row >= floor) & (row < code)).astype(jnp.float32).astype(jnp.bfloat16)
        inner = jnp.dot(before, feat_ref[3], preferred_element_type=jnp.float32)
        light = jnp.exp(-inner)
        own = row_ref[:, rows]
        pick = ((own >= start) & (own < start + base)).astype(jnp.float32).astype(jnp.bfloat16)
        for ch in range(4):
            value = feat_ref[ch, rows, :]
            if ch < 3:
                value = (value.astype(jnp.float32) * light).astype(jnp.bfloat16)
            sum_ref[ch] += jnp.dot(pick, value, preferred_element_type=jnp.float32)
        return carry

    lax.fori_loop(0, total // block, it, 0)
    for band in range(bands):
        for ch in range(4):
            value = sum_ref[ch, :, band * width:(band + 1) * width]
            pack_ref[:, band * 4 + ch, :] = value if ch < 3 else jnp.exp(-0.5 * value)
    out_ref[:, 0] = pack_ref[...].astype(out_ref.dtype)


def compose(row, col, got, made, view, views, count, bands, places, base):
    width = got.shape[2]
    total = row.shape[1]
    more = [] if made is None else [made]
    vmem = pl.BlockSpec(memory_space=pltpu.VMEM)
    return pl.pallas_call(
        functools.partial(compose_kernel, base=base, count=count),
        grid=(1,),
        in_specs=[vmem, vmem, vmem] + [pl.BlockSpec(memory_space=pl.ANY)] * len(more),
        out_specs=pl.BlockSpec((places, 1, bands * 4, width), lambda g: (0, view, 0, 0)),
        out_shape=jax.ShapeDtypeStruct((places, views, bands * 4, width), jnp.float32),
        scratch_shapes=[
            pltpu.VMEM((4, total, bands * width), jnp.bfloat16),
            pltpu.VMEM((4, places, bands * width), jnp.float32),
            pltpu.VMEM((places, bands * 4, width), jnp.float32),
        ],
        input_output_aliases={3: 0} if more else {},
        compiler_params=pltpu.CompilerParams(vmem_limit_bytes=32 << 20),
        name="compose",
    )(row, col, got, *more)


def exchange(parts):
    return lax.all_to_all(parts, AXES, split_axis=0, concat_axis=0, tiled=True)


def body(volume, resampler, ramp_slope, ramp_pivot, tile_owner, tile_cell, depth_order, slab_rank):
    count, edge = volume.shape[:2]
    views, _, cols = resampler.shape
    slabs, tiles = lax.axis_size("depth"), lax.axis_size("tile")
    devices = slabs * tiles
    cells_each = CELLS // slabs
    base = slabs * devices * count
    places = devices * cells_each
    bands, groups = max(1, edge // devices), max(1, devices // edge)
    width = cols // groups

    slab = lax.axis_index("depth").astype(jnp.int32).reshape(1)
    tags = (tile_owner.T, tile_cell.T, depth_order, slab_rank, slab)

    order = list(range(views))[::-1]
    made, codes = None, None
    for view in order:
        tagged = view == order[0]
        prints = render(volume, resampler, ramp_slope, ramp_pivot, tags, view, 0, count, bands, tagged)
        prints = prints.reshape(edge // bands, -1, groups, width).transpose(0, 2, 1, 3)
        got = exchange(prints.reshape(devices, -1, width))
        if tagged:
            digits = got[:, bands * 4 * count:bands * 4 * count + 3, :views * count].astype(jnp.int32)
            codes = digits[:, 0] + digits[:, 1] * 256 + digits[:, 2] * 65536
            codes = codes.reshape(devices, views, count).transpose(1, 0, 2).reshape(views, -1)
            floors = (codes // base) * base
        col = jnp.stack([codes[view], floors[view]], axis=1)
        made = compose(codes[view][None], col, got, made, view, views, count, bands, places, base)
    final = exchange(made.astype(jnp.float16).reshape(devices, cells_each * views, bands * 4, width))
    final = final.reshape(edge // bands, groups, cells_each, views, bands, 4, width)
    final = final.transpose(3, 5, 2, 0, 4, 1, 6).reshape(views, 4, cells_each * edge, cols)
    final = final.astype(jnp.float32)
    return final[:, :3, None], jnp.square(final[:, 3:])


def solution(mesh):
    in_specs = (
        P(AXES, None, None, None),
        P(),
        P(),
        P(),
        P(AXES, None),
        P(AXES, None),
        P(None, AXES),
        P(),
    )
    out_specs = (P(None, None, "tile", "depth", None), P(None, "tile", "depth", None))
    return jax.shard_map(body, mesh=mesh, in_specs=in_specs, out_specs=out_specs, check_vma=False)
```

```python
import functools

import jax
import jax.numpy as jnp
from jax import lax
from jax.experimental import pallas as pl
from jax.experimental.pallas import tpu as pltpu
from jax.sharding import PartitionSpec as P

LOG2E = 1.4426950408889634
GROUP = 16
STRIP = 16
CELLS = 8
TAGS = 8
AXES = ("depth", "tile")


def render_kernel(slope_ref, pivot_ref, owner_ref, cell_ref, order_ref, rank_ref, slab_ref, vol_ref, res_ref, out_ref, even_ref, odd_ref, ramp_ref, acc_ref, seen_ref, tint_ref, print_ref, *, view, count, tagged, tiles, bands):
    step = pl.program_id(0)
    bricks = count
    edge = vol_ref.shape[1]
    cols = res_ref.shape[2]
    pitch = edge + 1
    blocks = edge // GROUP
    strip = STRIP
    rate = -LOG2E / edge

    def multiply(block, samp_ref):
        weights = res_ref[0]
        if view == 0:
            rows = vol_ref[0, pl.ds(block * GROUP, GROUP)].reshape(GROUP * edge, edge)
            made = jnp.dot(rows, weights, preferred_element_type=jnp.float32)
            samp_ref[pl.ds(block * GROUP * edge, GROUP * edge), :] = made
        else:
            for j in range(GROUP):
                made = lax.dot_general(
                    vol_ref[0, block * GROUP + j], weights, (((0,), (0,)), ((), ())),
                    preferred_element_type=jnp.float32)
                samp_ref[pl.ds(block * GROUP * pitch + j * pitch, edge), :] = made

    def start():
        acc_ref[...] = jnp.zeros_like(acc_ref)
        seen_ref[...] = jnp.ones_like(seen_ref)
        tint_ref[...] = jnp.zeros_like(tint_ref)

    def ramps():
        for ch in range(3):
            gain = jnp.full((16, cols), 0.5 * slope_ref[ch], jnp.float32)
            offset = -gain * pivot_ref[ch]
            for place, value in ((0, gain), (1, offset)):
                debt = jnp.zeros_like(value)
                for j in range(GROUP):
                    want = value + debt
                    given = want.astype(jnp.bfloat16)
                    debt = want - given.astype(jnp.float32)
                    ramp_ref[j, ch, place] = given

    def march(block, samp_ref):
        for top in range(0, edge, strip):
            acc = acc_ref[pl.ds(top, strip), :]
            seen = seen_ref[pl.ds(top, strip), :]
            total = [None] * 3
            held = [None] * 3
            late = None
            for j in range(GROUP):
                if view == 0:
                    s = samp_ref[pl.ds((block * GROUP + j) * edge + top, strip), :]
                else:
                    s = samp_ref[pl.ds(top * pitch + block * GROUP + j, strip, stride=pitch), :]
                acc = acc + s
                left = jnp.exp2(acc * rate)
                w = (seen - left).astype(jnp.bfloat16)
                seen = left
                s16 = s.astype(jnp.bfloat16)
                tints = [jnp.tanh(s16 * ramp_ref[j, ch, 0] + ramp_ref[j, ch, 1]) for ch in range(3)]
                if late is not None:
                    take(total, held, j - 1, *late)
                late = (w, tints)
            take(total, held, GROUP - 1, *late)
            for ch in range(3):
                tint_ref[ch, pl.ds(top, strip), :] += total[ch].astype(jnp.float32)
            acc_ref[pl.ds(top, strip), :] = acc
            seen_ref[pl.ds(top, strip), :] = seen

    def take(total, held, j, w, tints):
        for ch in range(3):
            p = w * tints[ch]
            if j % 2 == 0:
                held[ch] = p
            else:
                p = held[ch] + p
                total[ch] = p if total[ch] is None else total[ch] + p

    def finish(brick):
        alpha = 1.0 - seen_ref[...]
        for ch in range(3):
            print_ref[pl.ds((ch * bricks + brick) * pitch, edge), :] = 0.5 * (alpha + tint_ref[ch])
        print_ref[pl.ds((3 * bricks + brick) * pitch, edge), :] = acc_ref[...] * (1.0 / edge)

    def loop(f):
        def it(block, carry):
            f(block)
            return carry
        lax.fori_loop(0, blocks, it, 0)

    @pl.when(step == 0)
    def _():
        ramps()
        loop(lambda block: multiply(block, even_ref))

    for parity, (own, other) in enumerate(((even_ref, odd_ref), (odd_ref, even_ref))):
        @pl.when((step > 0) & (step < bricks) & (lax.rem(step, 2) == parity))
        def _():
            start()

            def both(block):
                multiply(block, own)
                march(block, other)
            loop(both)
            finish(step - 1)

    last = odd_ref if count % 2 == 0 else even_ref

    @pl.when(step == bricks)
    def _():
        start()
        loop(lambda block: march(block, last))
        finish(step - 1)

        if tagged:
            views = order_ref.shape[0]
            slabs = rank_ref.shape[1]
            cells_each = CELLS // slabs
            bricks_all = slabs * tiles * count
            lane = lax.rem(lax.broadcasted_iota(jnp.int32, (TAGS, cols), 1), views * count)
            code = jnp.zeros((TAGS, cols), jnp.int32)
            for v in range(views):
                rank = rank_ref[v, slab_ref[0]]
                for b in range(count):
                    cell = cell_ref[v, b]
                    group = lax.div(cell, cells_each)
                    place = (group * tiles + owner_ref[v, b]) * cells_each + (cell - group * cells_each)
                    value = (place * slabs + rank) * bricks_all + order_ref[v, b]
                    code = jnp.where(lane == v * count + b, value, code)
            digit = lax.broadcasted_iota(jnp.int32, (TAGS, cols), 0)
            tags = jnp.where(digit == 0, code & 255, jnp.where(digit == 1, (code >> 8) & 255, code >> 16)).astype(jnp.float32)

        def swap(row, carry):
            for band in range(bands):
                part = print_ref[pl.ds(row * bands + band, 4 * bricks, stride=pitch), :]
                out_ref[row, band * 4 * bricks:(band + 1) * 4 * bricks, :] = part.astype(jnp.bfloat16)
            if tagged:
                out_ref[row, bands * 4 * bricks:, :] = tags.astype(jnp.bfloat16)
            return carry
        lax.fori_loop(0, edge // bands, swap, 0, unroll=2)


def render(volume, resampler, slope, pivot, tags, view, first, count, bands, tagged):
    edge, cols = volume.shape[1], resampler.shape[2]
    pitch = edge + 1
    slots = bands * 4 * count + (TAGS if tagged else 0)
    smem = pl.BlockSpec(memory_space=pltpu.SMEM)
    return pl.pallas_call(
        functools.partial(render_kernel, view=view, count=count, tagged=tagged, tiles=lax.axis_size("tile"), bands=bands),
        grid=(count + 1,),
        in_specs=[
            smem,
            smem,
        ] + [smem] * len(tags) + [
            pl.BlockSpec((1, edge, edge, edge), lambda g: (first + jnp.minimum(g, count - 1), 0, 0, 0)),
            pl.BlockSpec((1, edge, cols), lambda g: (view, 0, 0)),
        ],
        out_specs=pl.BlockSpec((edge // bands, slots, cols), lambda g: (0, 0, 0)),
        out_shape=jax.ShapeDtypeStruct((edge // bands, slots, cols), jnp.bfloat16),
        scratch_shapes=[
            pltpu.VMEM((edge * pitch, cols), jnp.float32),
            pltpu.VMEM((edge * pitch, cols), jnp.float32),
            pltpu.VMEM((GROUP, 3, 2, 16, cols), jnp.bfloat16),
            pltpu.VMEM((edge, cols), jnp.float32),
            pltpu.VMEM((edge, cols), jnp.float32),
            pltpu.VMEM((3, edge, cols), jnp.float32),
            pltpu.VMEM((4 * count * pitch, cols), jnp.float32),
        ],
        name=f"render{view}",
    )(slope, pivot, *tags, volume, resampler)


def compose_kernel(row_ref, col_ref, got_ref, *refs, base, count):
    out_ref, feat_ref, sum_ref, pack_ref = refs[-4:]
    total, lanes = feat_ref.shape[1:]
    places = sum_ref.shape[1]
    width = got_ref.shape[2]
    bands = lanes // width
    for band in range(bands):
        for ch in range(4):
            first = (band * 4 + ch) * count
            part = got_ref[:, first:first + count, :]
            feat_ref[ch, :, band * width:(band + 1) * width] = part.reshape(total, width)
    sum_ref[...] = jnp.zeros_like(sum_ref)
    block = min(256, total)
    row = row_ref[...]
    start = lax.broadcasted_iota(jnp.int32, (places, block), 0) * base

    def it(i, carry):
        rows = pl.ds(i * block, block)
        code = col_ref[rows, 0:1]
        floor = col_ref[rows, 1:2]
        before = ((row >= floor) & (row < code)).astype(jnp.float32).astype(jnp.bfloat16)
        inner = jnp.dot(before, feat_ref[3], preferred_element_type=jnp.float32)
        light = jnp.exp(-inner)
        own = row_ref[:, rows]
        pick = ((own >= start) & (own < start + base)).astype(jnp.float32).astype(jnp.bfloat16)
        for ch in range(4):
            value = feat_ref[ch, rows, :]
            if ch < 3:
                value = (value.astype(jnp.float32) * light).astype(jnp.bfloat16)
            sum_ref[ch] += jnp.dot(pick, value, preferred_element_type=jnp.float32)
        return carry

    lax.fori_loop(0, total // block, it, 0)
    for band in range(bands):
        for ch in range(4):
            value = sum_ref[ch, :, band * width:(band + 1) * width]
            pack_ref[:, band * 4 + ch, :] = value if ch < 3 else jnp.exp(-0.5 * value)
    out_ref[:, 0] = pack_ref[...].astype(out_ref.dtype)


def compose(row, col, got, made, view, views, count, bands, places, base):
    width = got.shape[2]
    total = row.shape[1]
    more = [] if made is None else [made]
    vmem = pl.BlockSpec(memory_space=pltpu.VMEM)
    return pl.pallas_call(
        functools.partial(compose_kernel, base=base, count=count),
        grid=(1,),
        in_specs=[vmem, vmem, vmem] + [pl.BlockSpec(memory_space=pl.ANY)] * len(more),
        out_specs=pl.BlockSpec((places, 1, bands * 4, width), lambda g: (0, view, 0, 0)),
        out_shape=jax.ShapeDtypeStruct((places, views, bands * 4, width), jnp.float32),
        scratch_shapes=[
            pltpu.VMEM((4, total, bands * width), jnp.bfloat16),
            pltpu.VMEM((4, places, bands * width), jnp.float32),
            pltpu.VMEM((places, bands * 4, width), jnp.float32),
        ],
        input_output_aliases={3: 0} if more else {},
        compiler_params=pltpu.CompilerParams(vmem_limit_bytes=32 << 20),
        name="compose",
    )(row, col, got, *more)


def exchange(parts):
    return lax.all_to_all(parts, AXES, split_axis=0, concat_axis=0, tiled=True)


def body(volume, resampler, ramp_slope, ramp_pivot, tile_owner, tile_cell, depth_order, slab_rank):
    count, edge = volume.shape[:2]
    views, _, cols = resampler.shape
    slabs, tiles = lax.axis_size("depth"), lax.axis_size("tile")
    devices = slabs * tiles
    cells_each = CELLS // slabs
    base = slabs * devices * count
    places = devices * cells_each
    bands, groups = max(1, edge // devices), max(1, devices // edge)
    width = cols // groups

    slab = lax.axis_index("depth").astype(jnp.int32).reshape(1)
    tags = (tile_owner.T, tile_cell.T, depth_order, slab_rank, slab)

    order = list(range(views))[::-1]
    made, codes = None, None
    for view in order:
        tagged = view == order[0]
        prints = render(volume, resampler, ramp_slope, ramp_pivot, tags, view, 0, count, bands, tagged)
        prints = prints.reshape(edge // bands, -1, groups, width).transpose(0, 2, 1, 3)
        got = exchange(prints.reshape(devices, -1, width))
        if tagged:
            digits = got[:, bands * 4 * count:bands * 4 * count + 3, :views * count].astype(jnp.int32)
            codes = digits[:, 0] + digits[:, 1] * 256 + digits[:, 2] * 65536
            codes = codes.reshape(devices, views, count).transpose(1, 0, 2).reshape(views, -1)
            floors = (codes // base) * base
        col = jnp.stack([codes[view], floors[view]], axis=1)
        made = compose(codes[view][None], col, got, made, view, views, count, bands, places, base)
    final = exchange(made.astype(jnp.float16).reshape(devices, cells_each * views, bands * 4, width))
    final = final.reshape(edge // bands, groups, cells_each, views, bands, 4, width)
    final = final.transpose(3, 5, 2, 0, 4, 1, 6).reshape(views, 4, cells_each * edge, cols)
    final = final.astype(jnp.float32)
    return final[:, :3, None], jnp.square(final[:, 3:])


def solution(mesh):
    in_specs = (
        P(AXES, None, None, None),
        P(),
        P(),
        P(),
        P(AXES, None),
        P(AXES, None),
        P(None, AXES),
        P(),
    )
    out_specs = (P(None, None, "tile", "depth", None), P(None, "tile", "depth", None))
    return jax.shard_map(body, mesh=mesh, in_specs=in_specs, out_specs=out_specs, check_vma=False)
```

```python
import functools

import jax
import jax.numpy as jnp
from jax import lax
from jax.experimental import pallas as pl
from jax.experimental.pallas import tpu as pltpu
from jax.sharding import PartitionSpec as P

LOG2E = 1.4426950408889634
GROUP = 16
STRIP = 16
CELLS = 8
TAGS = 8
AXES = ("depth", "tile")


def render_kernel(slope_ref, pivot_ref, owner_ref, cell_ref, order_ref, rank_ref, slab_ref, vol_ref, res_ref, out_ref, even_ref, odd_ref, ramp_ref, acc_ref, seen_ref, tint_ref, print_ref, tag_ref, *, view, count, tagged, tiles, bands):
    step = pl.program_id(0)
    bricks = count
    edge = vol_ref.shape[1]
    cols = res_ref.shape[2]
    pitch = edge + 1
    blocks = edge // GROUP
    strip = STRIP
    rate = -LOG2E / edge

    def multiply(block, samp_ref):
        weights = res_ref[0]
        if view == 0:
            rows = vol_ref[0, pl.ds(block * GROUP, GROUP)].reshape(GROUP * edge, edge)
            made = jnp.dot(rows, weights, preferred_element_type=jnp.float32)
            samp_ref[pl.ds(block * GROUP * edge, GROUP * edge), :] = made
        else:
            for j in range(GROUP):
                made = lax.dot_general(
                    vol_ref[0, block * GROUP + j], weights, (((0,), (0,)), ((), ())),
                    preferred_element_type=jnp.float32)
                samp_ref[pl.ds(block * GROUP * pitch + j * pitch, edge), :] = made

    def start():
        acc_ref[...] = jnp.zeros_like(acc_ref)
        seen_ref[...] = jnp.ones_like(seen_ref)
        tint_ref[...] = jnp.zeros_like(tint_ref)

    def ramps():
        for ch in range(3):
            gain = jnp.full((16, cols), 0.5 * slope_ref[ch], jnp.float32)
            offset = -gain * pivot_ref[ch]
            for place, value in ((0, gain), (1, offset)):
                debt = jnp.zeros_like(value)
                for j in range(GROUP):
                    want = value + debt
                    given = want.astype(jnp.bfloat16)
                    debt = want - given.astype(jnp.float32)
                    ramp_ref[j, ch, place] = given

    def codes():
        if tagged:
            views = order_ref.shape[0]
            slabs = rank_ref.shape[1]
            cells_each = CELLS // slabs
            bricks_all = slabs * tiles * count
            lane = lax.rem(lax.broadcasted_iota(jnp.int32, (TAGS, cols), 1), views * count)
            code = jnp.zeros((TAGS, cols), jnp.int32)
            for v in range(views):
                rank = rank_ref[v, slab_ref[0]]
                for b in range(count):
                    cell = cell_ref[v, b]
                    group = lax.div(cell, cells_each)
                    place = (group * tiles + owner_ref[v, b]) * cells_each + (cell - group * cells_each)
                    value = (place * slabs + rank) * bricks_all + order_ref[v, b]
                    code = jnp.where(lane == v * count + b, value, code)
            digit = lax.broadcasted_iota(jnp.int32, (TAGS, cols), 0)
            tag_ref[...] = jnp.where(digit == 0, code & 255, jnp.where(digit == 1, (code >> 8) & 255, code >> 16)).astype(jnp.float32)

    def march(block, samp_ref):
        for top in range(0, edge, strip):
            acc = acc_ref[pl.ds(top, strip), :]
            seen = seen_ref[pl.ds(top, strip), :]
            total = [None] * 3
            held = [None] * 3
            late = None
            for j in range(GROUP):
                if view == 0:
                    s = samp_ref[pl.ds((block * GROUP + j) * edge + top, strip), :]
                else:
                    s = samp_ref[pl.ds(top * pitch + block * GROUP + j, strip, stride=pitch), :]
                acc = acc + s
                left = jnp.exp2(acc * rate)
                w = (seen - left).astype(jnp.bfloat16)
                seen = left
                s16 = s.astype(jnp.bfloat16)
                tints = [jnp.tanh(s16 * ramp_ref[j, ch, 0] + ramp_ref[j, ch, 1]) for ch in range(3)]
                if late is not None:
                    take(total, held, j - 1, *late)
                late = (w, tints)
            take(total, held, GROUP - 1, *late)
            for ch in range(3):
                tint_ref[ch, pl.ds(top, strip), :] += total[ch].astype(jnp.float32)
            acc_ref[pl.ds(top, strip), :] = acc
            seen_ref[pl.ds(top, strip), :] = seen

    def take(total, held, j, w, tints):
        for ch in range(3):
            p = w * tints[ch]
            if j % 2 == 0:
                held[ch] = p
            else:
                p = held[ch] + p
                total[ch] = p if total[ch] is None else total[ch] + p

    def finish(brick):
        alpha = 1.0 - seen_ref[...]
        for ch in range(3):
            print_ref[pl.ds((ch * bricks + brick) * pitch, edge), :] = 0.5 * (alpha + tint_ref[ch])
        print_ref[pl.ds((3 * bricks + brick) * pitch, edge), :] = acc_ref[...] * (1.0 / edge)

    def loop(f):
        def it(block, carry):
            f(block)
            return carry
        lax.fori_loop(0, blocks, it, 0)

    @pl.when(step == 0)
    def _():
        ramps()
        codes()
        loop(lambda block: multiply(block, even_ref))

    for parity, (own, other) in enumerate(((even_ref, odd_ref), (odd_ref, even_ref))):
        @pl.when((step > 0) & (step < bricks) & (lax.rem(step, 2) == parity))
        def _():
            start()

            def both(block):
                multiply(block, own)
                march(block, other)
            loop(both)
            finish(step - 1)

    last = odd_ref if count % 2 == 0 else even_ref

    @pl.when(step == bricks)
    def _():
        start()
        loop(lambda block: march(block, last))
        finish(step - 1)

        def swap(row, carry):
            for band in range(bands):
                part = print_ref[pl.ds(row * bands + band, 4 * bricks, stride=pitch), :]
                out_ref[row, band * 4 * bricks:(band + 1) * 4 * bricks, :] = part.astype(jnp.bfloat16)
            if tagged:
                out_ref[row, bands * 4 * bricks:, :] = tag_ref[...].astype(jnp.bfloat16)
            return carry
        lax.fori_loop(0, edge // bands, swap, 0, unroll=8)


def render(volume, resampler, slope, pivot, tags, view, first, count, bands, tagged):
    edge, cols = volume.shape[1], resampler.shape[2]
    pitch = edge + 1
    slots = bands * 4 * count + (TAGS if tagged else 0)
    smem = pl.BlockSpec(memory_space=pltpu.SMEM)
    return pl.pallas_call(
        functools.partial(render_kernel, view=view, count=count, tagged=tagged, tiles=lax.axis_size("tile"), bands=bands),
        grid=(count + 1,),
        in_specs=[
            smem,
            smem,
        ] + [smem] * len(tags) + [
            pl.BlockSpec((1, edge, edge, edge), lambda g: (first + jnp.minimum(g, count - 1), 0, 0, 0)),
            pl.BlockSpec((1, edge, cols), lambda g: (view, 0, 0)),
        ],
        out_specs=pl.BlockSpec((edge // bands, slots, cols), lambda g: (0, 0, 0)),
        out_shape=jax.ShapeDtypeStruct((edge // bands, slots, cols), jnp.bfloat16),
        scratch_shapes=[
            pltpu.VMEM(((edge + 1) * pitch, cols), jnp.float32),
            pltpu.VMEM(((edge + 1) * pitch, cols), jnp.float32),
            pltpu.VMEM((GROUP, 3, 2, 16, cols), jnp.bfloat16),
            pltpu.VMEM((edge, cols), jnp.float32),
            pltpu.VMEM((edge, cols), jnp.float32),
            pltpu.VMEM((3, edge, cols), jnp.float32),
            pltpu.VMEM(((4 * count + 1) * pitch, cols), jnp.float32),
            pltpu.VMEM((TAGS, cols), jnp.float32),
        ],
        name=f"render{view}",
    )(slope, pivot, *tags, volume, resampler)


def compose_kernel(row_ref, col_ref, got_ref, *refs, base, count):
    out_ref, feat_ref, sum_ref, pack_ref = refs[-4:]
    total, lanes = feat_ref.shape[1:]
    places = sum_ref.shape[1]
    width = got_ref.shape[2]
    bands = lanes // width
    for band in range(bands):
        for ch in range(4):
            first = (band * 4 + ch) * count
            part = got_ref[:, first:first + count, :]
            feat_ref[ch, :, band * width:(band + 1) * width] = part.reshape(total, width)
    sum_ref[...] = jnp.zeros_like(sum_ref)
    block = min(256, total)
    row = row_ref[...]
    start = lax.broadcasted_iota(jnp.int32, (places, block), 0) * base

    def it(i, carry):
        rows = pl.ds(i * block, block)
        code = col_ref[rows, 0:1]
        floor = col_ref[rows, 1:2]
        before = ((row >= floor) & (row < code)).astype(jnp.float32).astype(jnp.bfloat16)
        inner = jnp.dot(before, feat_ref[3], preferred_element_type=jnp.float32)
        light = jnp.exp(-inner)
        own = row_ref[:, rows]
        pick = ((own >= start) & (own < start + base)).astype(jnp.float32).astype(jnp.bfloat16)
        for ch in range(4):
            value = feat_ref[ch, rows, :]
            if ch < 3:
                value = (value.astype(jnp.float32) * light).astype(jnp.bfloat16)
            sum_ref[ch] += jnp.dot(pick, value, preferred_element_type=jnp.float32)
        return carry

    lax.fori_loop(0, total // block, it, 0)
    for band in range(bands):
        for ch in range(4):
            value = sum_ref[ch, :, band * width:(band + 1) * width]
            pack_ref[:, band * 4 + ch, :] = value if ch < 3 else jnp.exp(-0.5 * value)
    out_ref[:, 0] = pack_ref[...].astype(out_ref.dtype)


def compose(row, col, got, made, view, views, count, bands, places, base):
    width = got.shape[2]
    total = row.shape[1]
    more = [] if made is None else [made]
    vmem = pl.BlockSpec(memory_space=pltpu.VMEM)
    return pl.pallas_call(
        functools.partial(compose_kernel, base=base, count=count),
        grid=(1,),
        in_specs=[vmem, vmem, vmem] + [pl.BlockSpec(memory_space=pl.ANY)] * len(more),
        out_specs=pl.BlockSpec((places, 1, bands * 4, width), lambda g: (0, view, 0, 0)),
        out_shape=jax.ShapeDtypeStruct((places, views, bands * 4, width), jnp.float32),
        scratch_shapes=[
            pltpu.VMEM((4, total, bands * width), jnp.bfloat16),
            pltpu.VMEM((4, places, bands * width), jnp.float32),
            pltpu.VMEM((places, bands * 4, width), jnp.float32),
        ],
        input_output_aliases={3: 0} if more else {},
        compiler_params=pltpu.CompilerParams(vmem_limit_bytes=32 << 20),
        name="compose",
    )(row, col, got, *more)


def exchange(parts):
    return lax.all_to_all(parts, AXES, split_axis=0, concat_axis=0, tiled=True)


def body(volume, resampler, ramp_slope, ramp_pivot, tile_owner, tile_cell, depth_order, slab_rank):
    count, edge = volume.shape[:2]
    views, _, cols = resampler.shape
    slabs, tiles = lax.axis_size("depth"), lax.axis_size("tile")
    devices = slabs * tiles
    cells_each = CELLS // slabs
    base = slabs * devices * count
    places = devices * cells_each
    bands, groups = max(1, edge // devices), max(1, devices // edge)
    width = cols // groups

    slab = lax.axis_index("depth").astype(jnp.int32).reshape(1)
    tags = (tile_owner.T, tile_cell.T, depth_order, slab_rank, slab)

    order = list(range(views))[::-1]
    made, codes = None, None
    for view in order:
        tagged = view == order[0]
        prints = render(volume, resampler, ramp_slope, ramp_pivot, tags, view, 0, count, bands, tagged)
        prints = prints.reshape(edge // bands, -1, groups, width).transpose(0, 2, 1, 3)
        got = exchange(prints.reshape(devices, -1, width))
        if tagged:
            digits = got[:, bands * 4 * count:bands * 4 * count + 3, :views * count].astype(jnp.int32)
            codes = digits[:, 0] + digits[:, 1] * 256 + digits[:, 2] * 65536
            codes = codes.reshape(devices, views, count).transpose(1, 0, 2).reshape(views, -1)
            floors = (codes // base) * base
        col = jnp.stack([codes[view], floors[view]], axis=1)
        made = compose(codes[view][None], col, got, made, view, views, count, bands, places, base)
    final = exchange(made.astype(jnp.float16).reshape(devices, cells_each * views, bands * 4, width))
    final = final.reshape(edge // bands, groups, cells_each, views, bands, 4, width)
    final = final.transpose(3, 5, 2, 0, 4, 1, 6).reshape(views, 4, cells_each * edge, cols)
    final = final.astype(jnp.float32)
    return final[:, :3, None], jnp.square(final[:, 3:])


def solution(mesh):
    in_specs = (
        P(AXES, None, None, None),
        P(),
        P(),
        P(),
        P(AXES, None),
        P(AXES, None),
        P(None, AXES),
        P(),
    )
    out_specs = (P(None, None, "tile", "depth", None), P(None, "tile", "depth", None))
    return jax.shard_map(body, mesh=mesh, in_specs=in_specs, out_specs=out_specs, check_vma=False)
```

```python
import functools

import jax
import jax.numpy as jnp
from jax import lax
from jax.experimental import pallas as pl
from jax.experimental.pallas import tpu as pltpu
from jax.sharding import PartitionSpec as P

LOG2E = 1.4426950408889634
GROUP = 16
STRIP = 16
CELLS = 8
TAGS = 8
AXES = ("depth", "tile")


def render_kernel(slope_ref, pivot_ref, owner_ref, cell_ref, order_ref, rank_ref, slab_ref, vol_ref, res_ref, out_ref, even_ref, odd_ref, ramp_ref, acc_ref, seen_ref, tint_ref, print_ref, tag_ref, *, view, count, tagged, tiles, bands):
    step = pl.program_id(0)
    bricks = count
    edge = vol_ref.shape[1]
    cols = res_ref.shape[2]
    pitch = edge + 1
    blocks = edge // GROUP
    strip = STRIP
    rate = -LOG2E / edge

    def multiply(block, samp_ref):
        weights = res_ref[0]
        if view == 0:
            rows = vol_ref[0, pl.ds(block * GROUP, GROUP)].reshape(GROUP * edge, edge)
            made = jnp.dot(rows, weights, preferred_element_type=jnp.float32)
            samp_ref[pl.ds(block * GROUP * edge, GROUP * edge), :] = made
        else:
            for j in range(GROUP):
                made = lax.dot_general(
                    vol_ref[0, block * GROUP + j], weights, (((0,), (0,)), ((), ())),
                    preferred_element_type=jnp.float32)
                samp_ref[pl.ds(block * GROUP * pitch + j * pitch, edge), :] = made

    def start():
        acc_ref[...] = jnp.zeros_like(acc_ref)
        seen_ref[...] = jnp.ones_like(seen_ref)
        tint_ref[...] = jnp.zeros_like(tint_ref)

    def ramps():
        for ch in range(3):
            gain = jnp.full((16, cols), 0.5 * slope_ref[ch], jnp.float32)
            offset = -gain * pivot_ref[ch]
            for place, value in ((0, gain), (1, offset)):
                debt = jnp.zeros_like(value)
                for j in range(GROUP):
                    want = value + debt
                    given = want.astype(jnp.bfloat16)
                    debt = want - given.astype(jnp.float32)
                    ramp_ref[j, ch, place] = given

    def codes():
        if tagged:
            views = order_ref.shape[0]
            slabs = rank_ref.shape[1]
            cells_each = CELLS // slabs
            bricks_all = slabs * tiles * count
            lane = lax.rem(lax.broadcasted_iota(jnp.int32, (TAGS, cols), 1), views * count)
            code = jnp.zeros((TAGS, cols), jnp.int32)
            for v in range(views):
                rank = rank_ref[v, slab_ref[0]]
                for b in range(count):
                    cell = cell_ref[v, b]
                    group = lax.div(cell, cells_each)
                    place = (group * tiles + owner_ref[v, b]) * cells_each + (cell - group * cells_each)
                    value = (place * slabs + rank) * bricks_all + order_ref[v, b]
                    code = jnp.where(lane == v * count + b, value, code)
            digit = lax.broadcasted_iota(jnp.int32, (TAGS, cols), 0)
            tag_ref[...] = jnp.where(digit == 0, code & 255, jnp.where(digit == 1, (code >> 8) & 255, code >> 16)).astype(jnp.float32)

    def march(block, samp_ref):
        for top in range(0, edge, strip):
            acc = acc_ref[pl.ds(top, strip), :]
            seen = seen_ref[pl.ds(top, strip), :]
            total = [None] * 3
            held = [None] * 3
            late = None
            for j in range(GROUP):
                if view == 0:
                    s = samp_ref[pl.ds((block * GROUP + j) * edge + top, strip), :]
                else:
                    s = samp_ref[pl.ds(top * pitch + block * GROUP + j, strip, stride=pitch), :]
                acc = acc + s
                left = jnp.exp2(acc * rate)
                w = (seen - left).astype(jnp.bfloat16)
                seen = left
                s16 = s.astype(jnp.bfloat16)
                tints = [jnp.tanh(s16 * ramp_ref[j, ch, 0] + ramp_ref[j, ch, 1]) for ch in range(3)]
                if late is not None:
                    take(total, held, j - 1, *late)
                late = (w, tints)
            take(total, held, GROUP - 1, *late)
            for ch in range(3):
                tint_ref[ch, pl.ds(top, strip), :] += total[ch].astype(jnp.float32)
            acc_ref[pl.ds(top, strip), :] = acc
            seen_ref[pl.ds(top, strip), :] = seen

    def take(total, held, j, w, tints):
        for ch in range(3):
            p = w * tints[ch]
            if j % 2 == 0:
                held[ch] = p
            else:
                p = held[ch] + p
                total[ch] = p if total[ch] is None else total[ch] + p

    def finish(brick):
        alpha = 1.0 - seen_ref[...]
        for ch in range(3):
            print_ref[pl.ds((ch * bricks + brick) * pitch, edge), :] = 0.5 * (alpha + tint_ref[ch])
        print_ref[pl.ds((3 * bricks + brick) * pitch, edge), :] = acc_ref[...] * (1.0 / edge)

    def loop(f):
        def it(block, carry):
            f(block)
            return carry
        lax.fori_loop(0, blocks, it, 0)

    @pl.when(step == 0)
    def _():
        ramps()
        codes()
        loop(lambda block: multiply(block, even_ref))

    for parity, (own, other) in enumerate(((even_ref, odd_ref), (odd_ref, even_ref))):
        @pl.when((step > 0) & (step < bricks) & (lax.rem(step, 2) == parity))
        def _():
            start()

            def both(block):
                multiply(block, own)
                march(block, other)
            loop(both)
            finish(step - 1)

    last = odd_ref if count % 2 == 0 else even_ref

    @pl.when(step == bricks)
    def _():
        start()
        loop(lambda block: march(block, last))
        finish(step - 1)

        def swap(row, carry):
            for band in range(bands):
                part = print_ref[pl.ds(row * bands + band, 4 * bricks, stride=pitch), :]
                out_ref[row, band * 4 * bricks:(band + 1) * 4 * bricks, :] = part.astype(jnp.bfloat16)
            if tagged:
                out_ref[row, bands * 4 * bricks:, :] = tag_ref[...].astype(jnp.bfloat16)
            return carry
        lax.fori_loop(0, edge // bands, swap, 0, unroll=8)


def render(volume, resampler, slope, pivot, tags, view, first, count, bands, tagged):
    edge, cols = volume.shape[1], resampler.shape[2]
    pitch = edge + 1
    slots = bands * 4 * count + (TAGS if tagged else 0)
    smem = pl.BlockSpec(memory_space=pltpu.SMEM)
    return pl.pallas_call(
        functools.partial(render_kernel, view=view, count=count, tagged=tagged, tiles=lax.axis_size("tile"), bands=bands),
        grid=(count + 1,),
        in_specs=[
            smem,
            smem,
        ] + [smem] * len(tags) + [
            pl.BlockSpec((1, edge, edge, edge), lambda g: (first + jnp.minimum(g, count - 1), 0, 0, 0)),
            pl.BlockSpec((1, edge, cols), lambda g: (view, 0, 0)),
        ],
        out_specs=pl.BlockSpec((edge // bands, slots, cols), lambda g: (0, 0, 0)),
        out_shape=jax.ShapeDtypeStruct((edge // bands, slots, cols), jnp.bfloat16),
        scratch_shapes=[
            pltpu.VMEM(((edge + 1) * pitch, cols), jnp.float32),
            pltpu.VMEM(((edge + 1) * pitch, cols), jnp.float32),
            pltpu.VMEM((GROUP, 3, 2, 16, cols), jnp.bfloat16),
            pltpu.VMEM((edge, cols), jnp.float32),
            pltpu.VMEM((edge, cols), jnp.float32),
            pltpu.VMEM((3, edge, cols), jnp.float32),
            pltpu.VMEM(((4 * count + 1) * pitch, cols), jnp.float32),
            pltpu.VMEM((TAGS, cols), jnp.float32),
        ],
        name=f"render{view}",
    )(slope, pivot, *tags, volume, resampler)


def compose_kernel(row_ref, col_ref, got_ref, *refs, base, count):
    out_ref, feat_ref, sum_ref, pack_ref = refs[-4:]
    total, lanes = feat_ref.shape[1:]
    places = sum_ref.shape[1]
    width = got_ref.shape[2]
    bands = lanes // width
    for band in range(bands):
        for ch in range(4):
            first = (band * 4 + ch) * count
            part = got_ref[:, first:first + count, :]
            feat_ref[ch, :, band * width:(band + 1) * width] = part.reshape(total, width)
    sum_ref[...] = jnp.zeros_like(sum_ref)
    block = min(256, total)
    row = row_ref[...]
    start = lax.broadcasted_iota(jnp.int32, (places, block), 0) * base

    def it(i, carry):
        rows = pl.ds(i * block, block)
        code = col_ref[rows, 0:1]
        floor = col_ref[rows, 1:2]
        before = ((row >= floor) & (row < code)).astype(jnp.float32).astype(jnp.bfloat16)
        inner = jnp.dot(before, feat_ref[3], preferred_element_type=jnp.float32)
        light = jnp.exp(-inner)
        own = row_ref[:, rows]
        pick = ((own >= start) & (own < start + base)).astype(jnp.float32).astype(jnp.bfloat16)
        for ch in range(4):
            value = feat_ref[ch, rows, :]
            if ch < 3:
                value = (value.astype(jnp.float32) * light).astype(jnp.bfloat16)
            sum_ref[ch] += jnp.dot(pick, value, preferred_element_type=jnp.float32)
        return carry

    lax.fori_loop(0, total // block, it, 0)
    for band in range(bands):
        for ch in range(4):
            value = sum_ref[ch, :, band * width:(band + 1) * width]
            pack_ref[:, band * 4 + ch, :] = value if ch < 3 else jnp.exp(-0.5 * value)
    out_ref[:, 0] = pack_ref[...].astype(out_ref.dtype)


def compose(row, col, got, made, view, views, count, bands, places, base):
    width = got.shape[2]
    total = row.shape[1]
    more = [] if made is None else [made]
    vmem = pl.BlockSpec(memory_space=pltpu.VMEM)
    return pl.pallas_call(
        functools.partial(compose_kernel, base=base, count=count),
        grid=(1,),
        in_specs=[vmem, vmem, vmem] + [pl.BlockSpec(memory_space=pl.ANY)] * len(more),
        out_specs=pl.BlockSpec((places, 1, bands * 4, width), lambda g: (0, view, 0, 0)),
        out_shape=jax.ShapeDtypeStruct((places, views, bands * 4, width), jnp.float32),
        scratch_shapes=[
            pltpu.VMEM((4, total, bands * width), jnp.bfloat16),
            pltpu.VMEM((4, places, bands * width), jnp.float32),
            pltpu.VMEM((places, bands * 4, width), jnp.float32),
        ],
        input_output_aliases={3: 0} if more else {},
        compiler_params=pltpu.CompilerParams(vmem_limit_bytes=32 << 20),
        name="compose",
    )(row, col, got, *more)


def exchange(parts):
    return lax.all_to_all(parts, AXES, split_axis=0, concat_axis=0, tiled=True)


def body(volume, resampler, ramp_slope, ramp_pivot, tile_owner, tile_cell, depth_order, slab_rank):
    count, edge = volume.shape[:2]
    views, _, cols = resampler.shape
    slabs, tiles = lax.axis_size("depth"), lax.axis_size("tile")
    devices = slabs * tiles
    cells_each = CELLS // slabs
    base = slabs * devices * count
    places = devices * cells_each
    bands, groups = max(1, edge // devices), max(1, devices // edge)
    width = cols // groups

    slab = lax.axis_index("depth").astype(jnp.int32).reshape(1)
    tags = (tile_owner.T, tile_cell.T, depth_order, slab_rank, slab)

    order = list(range(views))[::-1]
    made, codes = None, None
    for view in order:
        tagged = view == order[0]
        prints = render(volume, resampler, ramp_slope, ramp_pivot, tags, view, 0, count, bands, tagged)
        prints = prints.reshape(edge // bands, -1, groups, width).transpose(0, 2, 1, 3)
        got = exchange(prints.reshape(devices, -1, width))
        if tagged:
            digits = got[:, bands * 4 * count:bands * 4 * count + 3, :views * count].astype(jnp.int32)
            codes = digits[:, 0] + digits[:, 1] * 256 + digits[:, 2] * 65536
            codes = codes.reshape(devices, views, count).transpose(1, 0, 2).reshape(views, -1)
            floors = (codes // base) * base
        col = jnp.stack([codes[view], floors[view]], axis=1)
        made = compose(codes[view][None], col, got, made, view, views, count, bands, places, base)
    final = exchange(made.astype(jnp.float16).reshape(devices, cells_each * views, bands * 4, width))
    final = final.reshape(edge // bands, groups, cells_each, views, bands, 4, width)
    colour = final[..., :3, :].astype(jnp.float32).transpose(3, 5, 2, 0, 4, 1, 6)
    root = final[..., 3, :].astype(jnp.float32).transpose(3, 2, 0, 4, 1, 5)
    colour = colour.reshape(views, 3, 1, cells_each * edge, cols)
    return colour, jnp.square(root).reshape(views, 1, cells_each * edge, cols)


def solution(mesh):
    in_specs = (
        P(AXES, None, None, None),
        P(),
        P(),
        P(),
        P(AXES, None),
        P(AXES, None),
        P(None, AXES),
        P(),
    )
    out_specs = (P(None, None, "tile", "depth", None), P(None, "tile", "depth", None))
    return jax.shard_map(body, mesh=mesh, in_specs=in_specs, out_specs=out_specs, check_vma=False)
```
